768 devices in a mesh: lat: 96 (over y, z), lon: 8 (over x, core).
Axes of the slice: x: 4, y: 8, z: 12, core: 2. Of those that a mesh axis runs over, the one named last changes fastest.
Arguments:
- grid_in: float32 [196608, 512], P(('lat', 'lon')), may hold values from -6 to 6
- target: float32 [196608, 128], P(('lat', 'lon')), may hold values from -6 to 6
- w_enc: float32 [512, 512], replicated, may hold values from -0.25 to 0.25
- w_mix_self: float32 [2, 512, 512], replicated, may hold values from -0.25 to 0.25
- w_mix_nbr: float32 [2, 512, 512], replicated, may hold values from -0.25 to 0.25
- w_dec: float32 [512, 512], replicated, may hold values from -0.25 to 0.25
- w_out: float32 [512, 128], replicated, may hold values from -0.25 to 0.25
- var_weight: int32 [128], replicated, may hold values from 1 to 8
- g2m_idx: int32 [24576, 8], P(('lat', 'lon')), may hold values from 0 to 12287, as said below
- g2m_w: float32 [24576, 8], P(('lat', 'lon')), may hold values from 0.1 to 1
- mesh_nbr: int32 [24576, 6], P(('lat', 'lon')), may hold values from 0 to 24575, as said below
- m2g_idx: int32 [196608, 4], P(('lat', 'lon')), may hold values from 0 to 24575, as said below
- m2g_w: float32 [196608, 4], P(('lat', 'lon')), may hold values from 0.1 to 1
Outputs:
- pred: float32 [196608, 128], P(('lat', 'lon'))
- loss: float32 [], replicated
- grad_out: float32 [512, 128], replicated
The draws below stay inside these ranges and needn't reach their ends.
Inputs may be any that keep to these rules, and one draw needn't show every extreme that they name: `g2m_idx`: an entry of row r names a block held by a device whose lat index differs by at most one from that of the device holding row r, and whose lon index differs by at most one, counted cyclically over the 8 tiles; blocks of device d are rows d * 16 onward. `mesh_nbr`: an entry of row r names a mesh node held by a device whose lat index differs by at most one from that of the device holding row r, and whose lon index differs by at most one, counted cyclically over the 8 tiles. `m2g_idx`: an entry of row r names a mesh node held by a device whose lat index differs by at most one from that of the device holding row r, and whose lon index differs by at most one, counted cyclically over the 8 tiles.
All inputs are finite; a program needn't handle non-finite values.
Results may differ from the reference program's by a relative error of at most 0.00028.
Values sent between devices are 32-bit elements; how exact they have to be, the bound alone decides.
A program may use at most 32 MiB of HBM per device.

```python
import jax
import jax.numpy as jnp
from jax import lax

D = 512
V = 128
BS = 16
K = 8
K2 = 4
E = 6
L = 2
G_DEV = 256
MESH_DEV = 32
GRID = 196608
MESH = 24576
N_LAT = 96
N_LON = 8


def local_rows(key, rows, per_dev, source_dev, width):
    device = jnp.arange(rows, dtype=jnp.int32) // per_dev
    band = device // N_LON
    tile = device % N_LON
    key_a, key_b, key_c = jax.random.split(key, 3)
    offset = jax.random.randint(key_a, (rows, width), -1, 2, dtype=jnp.int32)
    src_band = jnp.clip(band[:, None] + offset, 0, N_LAT - 1)
    pick = jax.random.randint(key_b, (rows, width), 0, 5, dtype=jnp.int32)
    step = jnp.where(pick == 3, -1, jnp.where(pick == 4, 1, 0)).astype(jnp.int32)
    src_tile = (tile[:, None] + step + N_LON) % N_LON
    src_row = jax.random.randint(key_c, (rows, width), 0, source_dev, dtype=jnp.int32)
    return ((src_band * N_LON + src_tile) * source_dev + src_row).astype(jnp.int32)


def draw_g2m_idx(key, part):
    return local_rows(jax.random.fold_in(key, 11), MESH, MESH_DEV, G_DEV // BS, K)


def draw_mesh_nbr(key, part):
    return local_rows(jax.random.fold_in(key, 23), MESH, MESH_DEV, MESH_DEV, E)


def draw_m2g_idx(key, part):
    return local_rows(jax.random.fold_in(key, 37), GRID, G_DEV, MESH_DEV, K2)


def with_ends(values, key, smallest, high):
    longest = values.shape.index(max(values.shape))
    spots = []
    for shift in (0, 1):
        where = [jax.random.randint(jax.random.fold_in(key, axis), (), 0, length) for axis, length in enumerate(values.shape)]
        where[longest] = (where[longest] + shift) % values.shape[longest]
        spots.append(tuple(where))
    return values.at[spots[0]].set(smallest).at[spots[1]].set(high)


def level_of(own_key, shape, cuts, least, high):
    def one(dim, parts):
        heights = jax.random.uniform(jax.random.fold_in(jax.random.fold_in(own_key, 6), dim), (parts,), jnp.float32, least / len(cuts), high / len(cuts))
        return jnp.repeat(jnp.exp(heights), shape[dim] // parts).reshape((-1,) + (1,) * (len(shape) - dim - 1))

    factor_of = one(*cuts[0])
    for cut in cuts[1:]:
        factor_of = factor_of * one(*cut)
    return factor_of


def bell_draw(key, dims, scale, most, pieces=(), held_as=jnp.bfloat16):
    array = jax.random.normal(key, dims, jnp.float32) * scale
    if len(pieces) > 0:
        array = level_of(key, dims, pieces, -0.22, 0.18) * array
    return jnp.clip(array, min=-most, max=most).astype(held_as)


def setup_inputs(seed: int = 0) -> dict:
    keys = jax.random.split(jax.random.key(seed), 14)
    return {
        "grid_in": bell_draw(keys[0], (GRID, D), 1.0, 6.0, ((0, 768),), jnp.float32),
        "target": bell_draw(keys[1], (GRID, V), 1.0, 6.0, ((0, 768),), jnp.float32),
        "w_enc": bell_draw(keys[2], (D, D), D ** -0.5, 0.25, (), jnp.float32),
        "w_mix_self": bell_draw(keys[3], (L, D, D), D ** -0.5, 0.25, (), jnp.float32),
        "w_mix_nbr": bell_draw(keys[4], (L, D, D), D ** -0.5, 0.25, (), jnp.float32),
        "w_dec": bell_draw(keys[5], (D, D), D ** -0.5, 0.25, (), jnp.float32),
        "w_out": bell_draw(keys[6], (D, V), D ** -0.5, 0.25, (), jnp.float32),
        "var_weight": with_ends(jax.random.randint(keys[7], (V,), 1, 9), jax.random.fold_in(keys[7], 1), 1, 8).astype(jnp.int32),
        "g2m_idx": draw_g2m_idx(jax.random.fold_in(keys[13], 71), 0),
        "g2m_w": jnp.clip(0.1 + 0.9 * jax.random.uniform(keys[9], (MESH, K), jnp.float32) ** level_of(keys[9], (MESH, K), ((0, 768),), -0.2, 0.2), 0.1, 1.0),
        "mesh_nbr": draw_mesh_nbr(jax.random.fold_in(keys[13], 71), 0),
        "m2g_idx": draw_m2g_idx(jax.random.fold_in(keys[13], 71), 0),
        "m2g_w": jnp.clip(0.1 + 0.9 * jax.random.uniform(keys[12], (GRID, K2), jnp.float32) ** level_of(keys[12], (GRID, K2), ((0, 768),), -0.2, 0.2), 0.1, 1.0),
    }


def silu(value):
    return value / (1.0 + jnp.exp(-value))

def matmul(left, right):
    return jnp.dot(left, right, precision=lax.Precision.HIGHEST, preferred_element_type=jnp.float32)

def interp(table, index, weights):
    total = jnp.zeros((index.shape[0], table.shape[1]), jnp.float32)
    for slot in range(index.shape[1]):
        total = total + weights[:, slot:slot + 1] * jnp.take(table, index[:, slot], axis=0)
    return total / lax.optimization_barrier(jnp.sum(weights, axis=1, keepdims=True))

def mixing(mesh, mesh_nbr, self_weight, nbr_weight):
    agg = jnp.zeros_like(mesh)
    for slot in range(mesh_nbr.shape[1]):
        agg = agg + jnp.take(mesh, mesh_nbr[:, slot], axis=0)
    agg = agg / mesh_nbr.shape[1]
    center = mesh - lax.optimization_barrier(jnp.mean(mesh, axis=1, keepdims=True))
    nrm = center / jnp.sqrt(lax.optimization_barrier(jnp.mean(center * center, axis=1, keepdims=True)) + 1e-05)
    return mesh + silu(matmul(nrm, self_weight) + matmul(agg, nbr_weight))

def reference(grid_in, target, w_enc, w_mix_self, w_mix_nbr, w_dec, w_out, var_weight, g2m_idx, g2m_w, mesh_nbr, m2g_idx, m2g_w):
    h_one = grid_in + silu(matmul(grid_in, w_enc))
    blocks = lax.optimization_barrier(jnp.mean(h_one.reshape(-1, BS, D), axis=1))
    mesh = interp(blocks, g2m_idx, g2m_w)
    for layer in range(L):
        mesh = mixing(mesh, mesh_nbr, w_mix_self[layer], w_mix_nbr[layer])
    back = interp(mesh, m2g_idx, m2g_w)
    hidden = silu(matmul(h_one + back, w_dec))
    pred = matmul(hidden, w_out)
    scale = lax.optimization_barrier(jnp.sum(target * target, axis=0)) / GRID + 1e-06
    resid = pred - target
    err = lax.optimization_barrier(jnp.sum(resid * resid, axis=0))
    weights = var_weight.astype(jnp.float32)
    wsum = jnp.sum(weights)
    loss = jnp.sum(weights * err / (scale * GRID * wsum))
    coef = 2.0 * weights / (scale * GRID * wsum)
    grad_out = matmul(hidden.T, resid) * coef[None, :]
    return (pred, loss, grad_out)
```

```python
import functools

import jax
import jax.numpy as jnp
from jax import lax
from jax.experimental import pallas as pl
from jax.experimental.pallas import tpu as pltpu
from jax.sharding import PartitionSpec as P

BS = 16
L = 2
NZ = 12
EPS = 1e-05
F32 = jnp.float32
BF16 = jnp.bfloat16
MESH = pl.DeviceIdType.MESH


def split(value):
    high = value.astype(BF16)
    low = (value - high.astype(F32)).astype(BF16)
    return high, low


def dot(left, right):
    return jnp.dot(left, right, preferred_element_type=F32)


def mm3(left, right):
    (lh, ll), (rh, rl) = left, right
    return dot(lh, rh) + (dot(lh, rl) + dot(ll, rh))


def silu(value):
    return value / (1.0 + jnp.exp(-value))


def span(index, size):
    return pl.ds(pl.multiple_of(index * size, size), size)


def farthest_first(count):
    return sorted(range(count), key=lambda d: (-min(d, count - d), d))


def program_kernel(
    n_lat,
    n_lon,
    nz,
    grid_hbm,
    target_hbm,
    w_enc_hbm,
    w_self_hbm,
    w_nbr_hbm,
    w_dec_hbm,
    w_out_hbm,
    var_weight,
    g_idx_hbm,
    g_w_hbm,
    nbr_hbm,
    m_idx_hbm,
    m_w_hbm,
    pred_hbm,
    loss_ref,
    grad_hbm,
    grid,
    target,
    w_f32,
    w_out,
    g_idx,
    g_w,
    nbr,
    m_idx,
    m_w,
    w_bf,
    w_out_bf,
    h_bf,
    h_dec,
    back_bf,
    win0,
    win1,
    win2,
    win3,
    pred,
    grad,
    s1,
    s2_src,
    s2,
    s3,
    total,
    st1,
    st2,
    st3,
    in_sem,
    out_sem,
    halo_recv,
    halo_send,
    s1_recv,
    s4_recv,
    ar_recv,
    ar_send,
):
    lat = lax.axis_index("lat")
    lon = lax.axis_index("lon")
    ny = n_lat // nz
    y = lat // nz
    z = lat % nz
    points, width = grid.shape
    n_var = target.shape[1]
    piece = s3.shape[1]
    lon_rows = ny * piece
    grid_total = float(points * n_lat * n_lon)

    def at_lat(step):
        return ((lat + step + n_lat) % n_lat, lon)

    def at_lon(step):
        return (lat, (lon + step + n_lon) % n_lon)

    def at_y(step):
        return (((y + step) % ny) * nz + z, lon)

    def at_z(step):
        return (y * nz + (z + step) % nz, lon)

    peers = [at_lat(1), at_lat(-1)]
    peers += [at_lon(d) for d in range(1, n_lon)]
    peers += [at_y(d) for d in range(1, ny)]
    peers += [at_z(d) for d in range(1, nz)]

    barrier = pltpu.get_barrier_semaphore()
    for peer in peers:
        pl.semaphore_signal(barrier, inc=1, device_id=peer, device_id_type=MESH)

    def load(source, dest, slot):
        return pltpu.make_async_copy(source, dest, in_sem.at[slot])

    first = [
        load(g_idx_hbm, g_idx, 0),
        load(g_w_hbm, g_w, 1),
        load(grid_hbm, grid, 2),
        load(w_enc_hbm, w_f32.at[0], 3),
    ]
    later = [
        load(nbr_hbm, nbr, 4),
        load(m_idx_hbm, m_idx, 5),
        load(m_w_hbm, m_w, 6),
        load(w_dec_hbm, w_f32.at[1], 7),
        load(w_self_hbm.at[0], w_f32.at[2], 8),
        load(w_nbr_hbm.at[0], w_f32.at[3], 9),
        load(w_self_hbm.at[1], w_f32.at[4], 10),
        load(w_nbr_hbm.at[1], w_f32.at[5], 11),
        load(w_out_hbm, w_out, 12),
        load(target_hbm, target, 13),
    ]
    for copy in first:
        copy.start()

    def split_weight(which):
        def body(step, carry):
            rows = span(step, 64)
            high, low = split(w_f32[which, rows, :])
            w_bf[which, 0, rows, :] = high
            w_bf[which, 1, rows, :] = low
            return carry

        lax.fori_loop(0, width // 64, body, 0)

    def weight(which):
        return w_bf[which, 0], w_bf[which, 1]

    def locate(index, rows):
        shift = rows.bit_length() - 1
        lon_shift = n_lon.bit_length() - 1
        owner = index >> shift
        within = index & (rows - 1)
        band_slot = (owner >> lon_shift) - lat + 1
        tile_slot = ((owner & (n_lon - 1)) - lon + 1 + n_lon) & (n_lon - 1)
        return ((band_slot * 3 + tile_slot) << shift) + within

    def select(local, factors, columns):
        place = lax.broadcasted_iota(jnp.int32, (local.shape[0], columns), 1)
        chosen = jnp.zeros((local.shape[0], columns), F32)
        for k in range(local.shape[1]):
            value = 1.0 if factors is None else factors[:, k : k + 1]
            chosen = chosen + jnp.where(place == local[:, k : k + 1], value, 0.0)
        return chosen

    def send(win, rows, turn, source, dest, group, peer):
        pltpu.make_async_remote_copy(
            src_ref=win.at[pl.ds(source * rows, rows)],
            dst_ref=win.at[pl.ds(dest * rows, rows)],
            send_sem=halo_send.at[turn],
            recv_sem=halo_recv.at[turn, group],
            device_id=peer,
            device_id_type=MESH,
        ).start()

    def halo_start(win, rows, turn):
        send(win, rows, turn, 4, 1, 0, at_lat(1))
        send(win, rows, turn, 4, 7, 1, at_lat(-1))
        send(win, rows, turn, 4, 3, 2, at_lon(1))
        send(win, rows, turn, 4, 5, 2, at_lon(-1))

    def halo_wait(win, rows, turn, group, count):
        part = win.at[pl.ds(0, count * rows)]
        pltpu.make_async_copy(part, part, halo_recv.at[turn, group]).wait()

    def halo_forward(win, rows, turn):
        halo_wait(win, rows, turn, 0, 1)
        send(win, rows, turn, 1, 0, 3, at_lon(1))
        send(win, rows, turn, 1, 2, 3, at_lon(-1))
        halo_wait(win, rows, turn, 1, 1)
        send(win, rows, turn, 7, 6, 3, at_lon(1))
        send(win, rows, turn, 7, 8, 3, at_lon(-1))

    def halo_sent(win, rows, turn):
        part = win.at[pl.ds(0, 8 * rows)]
        pltpu.make_async_copy(part, part, halo_send.at[turn]).wait()

    blocks_dev = points // BS
    mesh_dev = nbr.shape[0]
    first[0].wait()
    first[1].wait()
    g_weights = g_w[...]
    g_select = split(select(locate(g_idx[...], blocks_dev), g_weights, 9 * blocks_dev))
    g_total = jnp.sum(g_weights, axis=1, keepdims=True)

    first[3].wait()
    for copy in later:
        copy.start()
    split_weight(0)
    first[2].wait()

    def encode(step, carry):
        rows = span(step, 128)
        value = grid[rows, :]
        h_one = value + silu(mm3(split(value), weight(0)))
        high, low = split(h_one)
        h_bf[0, rows, :] = high
        h_bf[1, rows, :] = low
        means = jnp.sum(h_one.reshape(128 // BS, BS, width), axis=1) * (1.0 / BS)
        start = pl.multiple_of(4 * blocks_dev + step * (128 // BS), 128 // BS)
        win0[pl.ds(start, 128 // BS), :] = means
        return carry

    lax.fori_loop(0, points // 128, encode, 0)
    pl.semaphore_wait(barrier, len(peers))
    halo_start(win0, blocks_dev, 0)

    later[0].wait()
    a_select = select(locate(nbr[...], mesh_dev), None, 9 * mesh_dev).astype(BF16)
    later[4].wait()
    split_weight(2)
    later[5].wait()
    split_weight(3)
    halo_forward(win0, blocks_dev, 0)
    later[3].wait()
    split_weight(1)

    def hidden_part(step, carry):
        rows = span(step, 128)
        h_dec[rows, :] = mm3((h_bf[0, rows, :], h_bf[1, rows, :]), weight(1))
        return carry

    lax.fori_loop(0, points // 128, hidden_part, 0)
    halo_wait(win0, blocks_dev, 0, 2, 2)
    halo_wait(win0, blocks_dev, 0, 3, 4)

    mesh = mm3(g_select, split(win0[...])) / g_total
    wins = (win1, win2, win3)

    def own(win):
        return pl.ds(4 * mesh_dev, mesh_dev)

    for layer in range(L):
        win = wins[layer]
        win[own(win), :] = mesh
        halo_start(win, mesh_dev, layer + 1)
        center = mesh - jnp.mean(mesh, axis=1, keepdims=True)
        spread = jnp.mean(center * center, axis=1, keepdims=True)
        nrm = center / jnp.sqrt(spread + EPS)
        self_part = mm3(split(nrm), weight(2 + 2 * layer))
        halo_forward(win, mesh_dev, layer + 1)
        if layer == 0:
            for slot, which in ((6, 4), (7, 5)):
                later[slot].wait()
                split_weight(which)
        else:
            later[1].wait()
            later[2].wait()

            def build(step, carry):
                rows = span(step, 64)
                factors = m_w[rows, :]
                factors = factors / jnp.sum(factors, axis=1, keepdims=True)
                chosen = select(locate(m_idx[rows, :], mesh_dev), factors, 9 * mesh_dev)
                high, low = split(chosen)
                back_bf[0, rows, :] = high
                back_bf[1, rows, :] = low
                return carry

            lax.fori_loop(0, points // 64, build, 0)
        halo_wait(win, mesh_dev, layer + 1, 2, 2)
        halo_wait(win, mesh_dev, layer + 1, 3, 4)
        high, low = split(win[...])
        agg = (dot(a_select, high) + dot(a_select, low)) / float(nbr.shape[1])
        mesh = mesh + silu(self_part + mm3(split(agg), weight(3 + 2 * layer)))

    win3[own(win3), :] = mm3(split(mesh), weight(1))
    halo_start(win3, mesh_dev, 3)
    later[8].wait()
    high, low = split(w_out[...])
    w_out_bf[0] = high
    w_out_bf[1] = low
    halo_forward(win3, mesh_dev, 3)
    later[9].wait()
    power = jnp.sum(target[...] * target[...], axis=0, keepdims=True)
    weights = var_weight[...].astype(F32)
    wsum = jnp.sum(weights, axis=1, keepdims=True)
    halo_wait(win3, mesh_dev, 3, 2, 2)
    halo_wait(win3, mesh_dev, 3, 3, 4)

    table = split(win3[...])
    w_out_parts = (w_out_bf[0], w_out_bf[1])
    err = jnp.zeros((1, n_var), F32)
    for step in range(points // 128):
        rows = pl.ds(step * 128, 128)
        hidden = silu(h_dec[rows, :] + mm3((back_bf[0, rows, :], back_bf[1, rows, :]), table))
        hh, hl = split(hidden)
        out = mm3((hh, hl), w_out_parts)
        pred[rows, :] = out
        resid = out - target[rows, :]
        err = err + jnp.sum(resid * resid, axis=0, keepdims=True)
        part = mm3((hh.T, hl.T), split(resid))
        if step == 0:
            grad[...] = part
        else:
            grad[...] += part
    pred_copy = pltpu.make_async_copy(pred, pred_hbm, out_sem.at[0])
    pred_copy.start()

    def push(source, dest, stage, recv, peer):
        pltpu.make_async_remote_copy(
            src_ref=source,
            dst_ref=dest,
            send_sem=ar_send.at[stage],
            recv_sem=recv,
            device_id=peer,
            device_id_type=MESH,
        ).start()

    def drain(part, sem):
        pltpu.make_async_copy(part, part, sem).wait()

    y_order = farthest_first(ny)
    lon_order = [d for d in farthest_first(n_lon) if d]
    z_order = [d for d in farthest_first(nz) if d]

    st1[lon] = jnp.concatenate([power, err], axis=0)
    for d in lon_order:
        push(st1.at[lon], st1.at[lon], 0, ar_recv.at[0], at_lon(d))
    for off in y_order:
        j = (y + off) % ny
        for d in lon_order:
            block = ((lon + d) % n_lon) * ny + j
            push(grad.at[span(block, piece)], s1.at[j, lon], 1, s1_recv.at[j], at_lon(d))

    drain(st1.at[pl.ds(0, n_lon - 1)], ar_recv.at[0])
    stats = st1[0]
    for i in range(1, n_lon):
        stats = stats + st1[i]
    st2[y] = stats
    for d in range(1, ny):
        push(st2.at[y], st2.at[y], 2, ar_recv.at[1], at_y(d))

    kept = None
    for off in y_order:
        j = (y + off) % ny
        drain(s1.at[j, pl.ds(0, n_lon - 1)], s1_recv.at[j])
        value = grad[span(lon * ny + j, piece), :]
        for d in range(1, n_lon):
            value = value + s1[j, (lon + d) % n_lon]
        if off:
            s2_src[j] = value
            push(s2_src.at[j], s2.at[y], 3, ar_recv.at[2], at_y(off))
        else:
            kept = value

    drain(st2.at[pl.ds(0, ny - 1)], ar_recv.at[1])
    stats = st2[0]
    for i in range(1, ny):
        stats = stats + st2[i]
    st3[z] = stats
    for d in z_order:
        push(st3.at[z], st3.at[z], 4, ar_recv.at[3], at_z(d))

    drain(s2.at[pl.ds(0, ny - 1)], ar_recv.at[2])
    for off in range(1, ny):
        kept = kept + s2[(y + off) % ny]
    s3[z] = kept
    for d in z_order:
        push(s3.at[z], s3.at[z], 5, ar_recv.at[4], at_z(d))

    drain(st3.at[pl.ds(0, nz - 1)], ar_recv.at[3])
    stats = st3[0]
    for i in range(1, nz):
        stats = stats + st3[i]
    scale = stats[0:1] / grid_total + 1e-06
    norm = scale * grid_total * wsum
    loss = jnp.sum(weights * stats[1:2] / norm, axis=1, keepdims=True)
    loss_ref[...] = jnp.broadcast_to(loss, loss_ref.shape)
    coef = 2.0 * weights / norm

    drain(s3.at[pl.ds(0, nz - 1)], ar_recv.at[4])
    value = s3[0]
    for i in range(1, nz):
        value = value + s3[i]
    mine = span(lon * ny + y, piece)
    total[mine, :] = value * coef
    for off in y_order:
        if off:
            push(total.at[mine], total.at[mine], 6, s4_recv.at[y], at_y(off))
    for d in lon_order:
        push(total.at[mine], total.at[mine], 7, ar_recv.at[5], at_lon(d))
    for off in reversed(y_order):
        if off:
            j = (y + off) % ny
            block = span(lon * ny + j, piece)
            drain(total.at[block], s4_recv.at[j])
            for d in lon_order:
                push(total.at[block], total.at[block], 7, ar_recv.at[5], at_lon(d))
    drain(total.at[pl.ds(0, (n_lon - 1) * lon_rows)], ar_recv.at[5])
    grad_copy = pltpu.make_async_copy(total, grad_hbm, out_sem.at[1])
    grad_copy.start()

    halo_sent(win0, blocks_dev, 0)
    for turn, win in enumerate(wins):
        halo_sent(win, mesh_dev, turn + 1)
    drain(st1.at[pl.ds(0, n_lon - 1)], ar_send.at[0])
    drain(grad.at[pl.ds(0, (n_lon - 1) * lon_rows)], ar_send.at[1])
    drain(st2.at[pl.ds(0, ny - 1)], ar_send.at[2])
    drain(s2.at[pl.ds(0, ny - 1)], ar_send.at[3])
    drain(st3.at[pl.ds(0, nz - 1)], ar_send.at[4])
    drain(s3.at[pl.ds(0, nz - 1)], ar_send.at[5])
    drain(total.at[pl.ds(0, (ny - 1) * piece)], ar_send.at[6])
    drain(total.at[pl.ds(0, (n_lon - 1) * lon_rows)], ar_send.at[7])
    pred_copy.wait()
    grad_copy.wait()


def shards(
    nz,
    grid_in,
    target,
    w_enc,
    w_mix_self,
    w_mix_nbr,
    w_dec,
    w_out,
    var_weight,
    g2m_idx,
    g2m_w,
    mesh_nbr,
    m2g_idx,
    m2g_w,
):
    n_lat = lax.axis_size("lat")
    n_lon = lax.axis_size("lon")
    ny = n_lat // nz
    points, width = grid_in.shape
    n_var = target.shape[1]
    mesh_dev = mesh_nbr.shape[0]
    blocks_dev = points // BS
    piece = width // (n_lon * ny)
    window = 9 * mesh_dev
    hbm = pl.BlockSpec(memory_space=pl.ANY)
    vmem = pl.BlockSpec(memory_space=pltpu.VMEM)
    pred, loss, grad = pl.pallas_call(
        functools.partial(program_kernel, n_lat, n_lon, nz),
        name="forecast_step",
        out_shape=(
            jax.ShapeDtypeStruct((points, n_var), F32),
            jax.ShapeDtypeStruct((1, n_var), F32),
            jax.ShapeDtypeStruct((width, n_var), F32),
        ),
        in_specs=[hbm] * 7 + [vmem] + [hbm] * 5,
        out_specs=(hbm, vmem, hbm),
        scratch_shapes=[
            pltpu.VMEM((points, width), F32),
            pltpu.VMEM((points, n_var), F32),
            pltpu.VMEM((6, width, width), F32),
            pltpu.VMEM((width, n_var), F32),
            pltpu.VMEM(g2m_idx.shape, jnp.int32),
            pltpu.VMEM(g2m_w.shape, F32),
            pltpu.VMEM(mesh_nbr.shape, jnp.int32),
            pltpu.VMEM(m2g_idx.shape, jnp.int32),
            pltpu.VMEM(m2g_w.shape, F32),
            pltpu.VMEM((6, 2, width, width), BF16),
            pltpu.VMEM((2, width, n_var), BF16),
            pltpu.VMEM((2, points, width), BF16),
            pltpu.VMEM((points, width), F32),
            pltpu.VMEM((2, points, window), BF16),
            pltpu.VMEM((9 * blocks_dev, width), F32),
            pltpu.VMEM((window, width), F32),
            pltpu.VMEM((window, width), F32),
            pltpu.VMEM((window, width), F32),
            pltpu.VMEM((points, n_var), F32),
            pltpu.VMEM((width, n_var), F32),
            pltpu.VMEM((ny, n_lon, piece, n_var), F32),
            pltpu.VMEM((ny, piece, n_var), F32),
            pltpu.VMEM((ny, piece, n_var), F32),
            pltpu.VMEM((nz, piece, n_var), F32),
            pltpu.VMEM((width, n_var), F32),
            pltpu.VMEM((n_lon, 2, n_var), F32),
            pltpu.VMEM((ny, 2, n_var), F32),
            pltpu.VMEM((nz, 2, n_var), F32),
            pltpu.SemaphoreType.DMA((14,)),
            pltpu.SemaphoreType.DMA((2,)),
            pltpu.SemaphoreType.DMA((4, 4)),
            pltpu.SemaphoreType.DMA((4,)),
            pltpu.SemaphoreType.DMA((ny,)),
            pltpu.SemaphoreType.DMA((ny,)),
            pltpu.SemaphoreType.DMA((6,)),
            pltpu.SemaphoreType.DMA((8,)),
        ],
        compiler_params=pltpu.CompilerParams(collective_id=0, has_side_effects=True),
    )(
        grid_in,
        target,
        w_enc,
        w_mix_self,
        w_mix_nbr,
        w_dec,
        w_out,
        var_weight.reshape(1, n_var),
        g2m_idx,
        g2m_w,
        mesh_nbr,
        m2g_idx,
        m2g_w,
    )
    return (pred, loss[0, 0], grad)


def solution(mesh, nz=NZ):
    rows = P(("lat", "lon"), None)
    placed = (rows, rows, P(), P(), P(), P(), P(), P(), rows, rows, rows, rows, rows)
    return jax.shard_map(
        functools.partial(shards, nz),
        mesh=mesh,
        in_specs=placed,
        out_specs=(rows, P(), P()),
        check_vma=False,
    )
```

```python
import functools

import jax
import jax.numpy as jnp
from jax import lax
from jax.experimental import pallas as pl
from jax.experimental.pallas import tpu as pltpu
from jax.sharding import PartitionSpec as P

BS = 16
L = 2
NZ = 12
EPS = 1e-05
F32 = jnp.float32
BF16 = jnp.bfloat16
MESH = pl.DeviceIdType.MESH


def split(value):
    high = value.astype(BF16)
    low = (value - high.astype(F32)).astype(BF16)
    return high, low


def dot(left, right):
    return jnp.dot(left, right, preferred_element_type=F32)


def mm3(left, right):
    (lh, ll), (rh, rl) = left, right
    rows = lh.shape[0]
    both = dot(jnp.concatenate([lh, ll], axis=0), rh)
    return both[:rows] + (both[rows:] + dot(lh, rl))


def silu(value):
    return value / (1.0 + jnp.exp(-value))


def span(index, size):
    return pl.ds(pl.multiple_of(index * size, size), size)


def program_kernel(
    n_lat,
    n_lon,
    nz,
    grid_hbm,
    target_hbm,
    w_enc_hbm,
    w_self_hbm,
    w_nbr_hbm,
    w_dec_hbm,
    w_out_hbm,
    var_weight,
    g_idx_hbm,
    g_w_hbm,
    nbr_hbm,
    m_idx_hbm,
    m_w_hbm,
    pred_hbm,
    loss_ref,
    grad_hbm,
    grid,
    target,
    w_f32,
    w_out,
    g_idx,
    g_w,
    nbr,
    m_idx,
    m_w,
    m_idx_cols,
    m_w_cols,
    w_bf,
    w_out_bf,
    h_bf,
    h_dec,
    back_bf,
    win0,
    win1,
    win2,
    win3,
    pred,
    grad,
    half,
    s1_src,
    s1,
    s2,
    total,
    st0,
    st1,
    st2,
    in_sem,
    out_sem,
    halo_recv,
    halo_send,
    half_recv,
    part_recv,
    ar_recv,
    ar_send,
):
    lat = lax.axis_index("lat")
    lon = lax.axis_index("lon")
    ny = n_lat // nz
    y = lat // nz
    z = lat % nz
    points, width = grid.shape
    n_var = target.shape[1]
    piece = s2.shape[1]
    nx = n_lon // 2
    x = lon // 2
    core = lon % 2
    x_rows = ny * piece
    half_rows = nx * x_rows
    grid_total = float(points * n_lat * n_lon)

    inner = 1 - 2 * core
    outer = -inner

    def near(lat_step, lon_step):
        return ((lat + lat_step + n_lat) % n_lat, (lon + lon_step + n_lon) % n_lon)

    def at_xy(dx, dy):
        return (((y + dy) % ny) * nz + z, ((x + dx) % nx) * 2 + core)

    def at_z(step):
        return (y * nz + (z + step) % nz, lon)

    def ring(count):
        return sorted(range(count), key=lambda d: (-min(d, count - d), d))

    xy_order = [(dx, dy) for dx in range(nx) for dy in range(ny) if dx or dy]
    xy_order.sort(key=lambda d: -(min(d[0], nx - d[0]) + min(d[1], ny - d[1])))
    z_order = [d for d in ring(nz) if d]

    peers = [near(1, 0), near(-1, 0), near(1, outer), near(-1, outer), near(0, outer), near(0, inner)]
    peers += [at_xy(dx, dy) for dx, dy in xy_order]
    peers += [at_z(d) for d in z_order]

    barrier = pltpu.get_barrier_semaphore()
    for peer in peers:
        pl.semaphore_signal(barrier, inc=1, device_id=peer, device_id_type=MESH)

    def load(source, dest, slot):
        return pltpu.make_async_copy(source, dest, in_sem.at[slot])

    quarter = width // 4
    first = [
        load(w_enc_hbm.at[pl.ds(q * quarter, quarter)], w_f32.at[0, pl.ds(q * quarter, quarter)], q)
        for q in range(4)
    ]
    first += [
        load(grid_hbm.at[pl.ds(q * 128, 128)], grid.at[pl.ds(q * 128, 128)], 4 + q)
        for q in range(points // 128)
    ]
    later = [
        load(nbr_hbm, nbr, 6),
        load(m_idx_hbm, m_idx, 7),
        load(m_w_hbm, m_w, 8),
        load(w_dec_hbm, w_f32.at[1], 9),
        load(w_self_hbm.at[0], w_f32.at[2], 10),
        load(w_nbr_hbm.at[0], w_f32.at[3], 11),
        load(w_self_hbm.at[1], w_f32.at[4], 12),
        load(w_nbr_hbm.at[1], w_f32.at[5], 13),
        load(w_out_hbm, w_out, 14),
        load(target_hbm, target, 15),
        load(g_idx_hbm, g_idx, 16),
        load(g_w_hbm, g_w, 17),
    ]
    for copy in first:
        copy.start()

    def split_weight(which, start=0, count=8):
        def body(step, carry):
            rows = span(step, width // 8)
            high, low = split(w_f32[which, rows, :])
            w_bf[which, 0, rows, :] = high
            w_bf[which, 1, rows, :] = low
            return carry

        lax.fori_loop(start, start + count, body, 0)

    def weight(which):
        return w_bf[which, 0], w_bf[which, 1]

    def locate(index, rows):
        shift = rows.bit_length() - 1
        lon_shift = n_lon.bit_length() - 1
        owner = index >> shift
        within = index & (rows - 1)
        band_slot = (owner >> lon_shift) - lat + 1
        tile_slot = ((owner & (n_lon - 1)) - lon + 1 + n_lon) & (n_lon - 1)
        return ((band_slot * 3 + tile_slot) << shift) + within

    def select(local, factors, columns):
        place = lax.broadcasted_iota(jnp.int32, (local.shape[0], columns), 1)
        chosen = jnp.zeros((local.shape[0], columns), F32)
        for k in range(local.shape[1]):
            value = 1.0 if factors is None else factors[:, k : k + 1]
            chosen = chosen + jnp.where(place == local[:, k : k + 1], value, 0.0)
        return chosen

    def send(win, rows, turn, source, dest, group, peer):
        pltpu.make_async_remote_copy(
            src_ref=win.at[span(source, rows)],
            dst_ref=win.at[span(dest, rows)],
            send_sem=halo_send.at[turn],
            recv_sem=halo_recv.at[turn, group],
            device_id=peer,
            device_id_type=MESH,
        ).start()

    def slot(lat_step, lon_step):
        return (lat_step + 1) * 3 + lon_step + 1

    def halo_start(win, rows, turn):
        for step, group in ((1, 0), (-1, 1)):
            send(win, rows, turn, 4, slot(-step, 0), group, near(step, 0))
        for step in (1, -1):
            send(win, rows, turn, 4, slot(-step, -outer), 2, near(step, outer))
        send(win, rows, turn, 4, slot(0, -outer), 2, near(0, outer))
        send(win, rows, turn, 4, slot(0, -inner), 2, near(0, inner))

    def halo_wait(win, rows, turn, group, count):
        part = win.at[pl.ds(0, count * rows)]
        pltpu.make_async_copy(part, part, halo_recv.at[turn, group]).wait()

    def halo_forward(win, rows, turn):
        for step, group in ((-1, 0), (1, 1)):
            halo_wait(win, rows, turn, group, 1)
            send(win, rows, turn, slot(step, 0), slot(step, -inner), 2, near(0, inner))

    def halo_sent(win, rows, turn):
        part = win.at[pl.ds(0, 8 * rows)]
        pltpu.make_async_copy(part, part, halo_send.at[turn]).wait()

    blocks_dev = points // BS
    mesh_dev = nbr.shape[1]
    for q in range(4):
        first[q].wait()
        split_weight(0, 2 * q, 2)
    for copy in later:
        copy.start()
    for copy in first[4:]:
        copy.wait()

    def encode(step, carry):
        rows = span(step, 128)
        value = grid[rows, :]
        h_one = value + silu(mm3(split(value), weight(0)))
        high, low = split(h_one)
        h_bf[0, rows, :] = high
        h_bf[1, rows, :] = low
        means = jnp.sum(h_one.reshape(128 // BS, BS, width), axis=1) * (1.0 / BS)
        start = pl.multiple_of(4 * blocks_dev + step * (128 // BS), 128 // BS)
        win0[pl.ds(start, 128 // BS), :] = means
        return carry

    lax.fori_loop(0, points // 128, encode, 0)
    pl.semaphore_wait(barrier, len(peers))
    halo_start(win0, blocks_dev, 0)

    later[10].wait()
    later[11].wait()
    g_weights = g_w[...].T
    g_local = locate(g_idx[...].T, blocks_dev)
    g_select = split(select(g_local, g_weights, 9 * blocks_dev))
    g_total = jnp.sum(g_weights, axis=1, keepdims=True)
    later[0].wait()
    a_select = select(locate(nbr[...].T, mesh_dev), None, 9 * mesh_dev).astype(BF16)
    later[4].wait()
    split_weight(2)
    later[5].wait()
    split_weight(3)
    later[3].wait()
    split_weight(1)
    halo_forward(win0, blocks_dev, 0)

    def hidden_part(step, carry):
        rows = span(step, 128)
        h_dec[rows, :] = mm3((h_bf[0, rows, :], h_bf[1, rows, :]), weight(1))
        return carry

    lax.fori_loop(0, points // 128, hidden_part, 0)
    halo_wait(win0, blocks_dev, 0, 2, 6)

    mesh = mm3(g_select, split(win0[...])) / g_total
    wins = (win1, win2, win3)

    def own(win):
        return pl.ds(4 * mesh_dev, mesh_dev)

    for layer in range(L):
        win = wins[layer]
        win[own(win), :] = mesh
        halo_start(win, mesh_dev, layer + 1)
        center = mesh - jnp.mean(mesh, axis=1, keepdims=True)
        spread = jnp.mean(center * center, axis=1, keepdims=True)
        nrm = center / jnp.sqrt(spread + EPS)
        self_part = mm3(split(nrm), weight(2 + 2 * layer))
        halo_forward(win, mesh_dev, layer + 1)
        if layer == 0:
            for ready, which in ((6, 4), (7, 5)):
                later[ready].wait()
                split_weight(which)
        else:
            later[1].wait()
            later[2].wait()

            factors = m_w[...].T
            factors = factors / jnp.sum(factors, axis=1, keepdims=True)
            m_w_cols[...] = factors
            m_idx_cols[...] = locate(m_idx[...].T, mesh_dev)

            def build(step, carry):
                rows = span(step, 64)
                chosen = select(m_idx_cols[rows, :], m_w_cols[rows, :], 9 * mesh_dev)
                high, low = split(chosen)
                back_bf[0, rows, :] = high
                back_bf[1, rows, :] = low
                return carry

            lax.fori_loop(0, points // 64, build, 0)
        halo_wait(win, mesh_dev, layer + 1, 2, 6)
        high, low = split(win[...])
        agg = (dot(a_select, high) + dot(a_select, low)) / float(nbr.shape[0])
        mesh = mesh + silu(self_part + mm3(split(agg), weight(3 + 2 * layer)))

    win3[own(win3), :] = mm3(split(mesh), weight(1))
    halo_start(win3, mesh_dev, 3)
    later[8].wait()
    high, low = split(w_out[...])
    w_out_bf[0] = high
    w_out_bf[1] = low
    halo_forward(win3, mesh_dev, 3)
    later[9].wait()
    power = jnp.sum(target[...] * target[...], axis=0, keepdims=True)
    weights = var_weight[...].astype(F32)
    wsum = jnp.sum(weights, axis=1, keepdims=True)
    halo_wait(win3, mesh_dev, 3, 2, 6)

    table = split(win3[...])
    w_out_parts = (w_out_bf[0], w_out_bf[1])
    err = jnp.zeros((1, n_var), F32)
    for step in range(points // 128):
        rows = pl.ds(step * 128, 128)
        hidden = silu(h_dec[rows, :] + mm3((back_bf[0, rows, :], back_bf[1, rows, :]), table))
        hh, hl = split(hidden)
        out = mm3((hh, hl), w_out_parts)
        pred[rows, :] = out
        resid = out - target[rows, :]
        err = err + jnp.sum(resid * resid, axis=0, keepdims=True)
        part = mm3((hh.T, hl.T), split(resid))
        if step == 0:
            grad[...] = part
        else:
            grad[...] += part
    pred_copy = pltpu.make_async_copy(pred, pred_hbm, out_sem.at[0])
    pred_copy.start()

    def push(source, dest, stage, recv, peer):
        pltpu.make_async_remote_copy(
            src_ref=source,
            dst_ref=dest,
            send_sem=ar_send.at[stage],
            recv_sem=recv,
            device_id=peer,
            device_id_type=MESH,
        ).start()

    def drain(part, sem):
        pltpu.make_async_copy(part, part, sem).wait()

    partner = near(0, inner)
    me = x * ny + y
    keep_row = core * half_rows

    st0[core] = jnp.concatenate([power, err], axis=0)
    push(st0.at[core], st0.at[core], 0, ar_recv.at[0], partner)
    for dx in ring(nx):
        bx = (x + dx) % nx
        rows = pl.ds(pl.multiple_of((1 - core) * half_rows + bx * x_rows, x_rows), x_rows)
        push(grad.at[rows], half.at[span(bx, x_rows)], 1, half_recv.at[bx], partner)

    drain(st0.at[pl.ds(0, 1)], ar_recv.at[0])
    st1[me] = st0[0] + st0[1]
    for dx, dy in xy_order:
        push(st1.at[me], st1.at[me], 2, ar_recv.at[1], at_xy(dx, dy))
    for dx in ring(nx):
        bx = (x + dx) % nx
        drain(half.at[span(bx, x_rows)], half_recv.at[bx])
        rows = pl.ds(pl.multiple_of(keep_row + bx * x_rows, x_rows), x_rows)
        s1_src[span(bx, x_rows), :] = grad[rows, :] + half[span(bx, x_rows), :]
        for dy in ring(ny):
            if dx or dy:
                block = bx * ny + (y + dy) % ny
                push(s1_src.at[span(block, piece)], s1.at[me], 3, ar_recv.at[2], at_xy(dx, dy))
    s1[me] = s1_src[span(me, piece), :]

    others = nx * ny - 1
    drain(st1.at[pl.ds(0, others)], ar_recv.at[1])
    st2[z] = jnp.sum(st1[...], axis=0)
    for d in z_order:
        push(st2.at[z], st2.at[z], 4, ar_recv.at[3], at_z(d))
    drain(s1.at[pl.ds(0, others)], ar_recv.at[2])
    s2[z] = jnp.sum(s1[...], axis=0)
    for d in z_order:
        push(s2.at[z], s2.at[z], 5, ar_recv.at[4], at_z(d))

    drain(st2.at[pl.ds(0, nz - 1)], ar_recv.at[3])
    stats = jnp.sum(st2[...], axis=0)
    scale = stats[0:1] / grid_total + 1e-06
    norm = scale * grid_total * wsum
    loss = jnp.sum(weights * stats[1:2] / norm, axis=1, keepdims=True)
    loss_ref[...] = jnp.broadcast_to(loss, loss_ref.shape)
    coef = 2.0 * weights / norm

    drain(s2.at[pl.ds(0, nz - 1)], ar_recv.at[4])
    mine = pl.ds(pl.multiple_of(keep_row + me * piece, piece), piece)
    total[mine, :] = jnp.sum(s2[...], axis=0) * coef
    for dx, dy in xy_order:
        push(total.at[mine], total.at[mine], 6, part_recv.at[x], at_xy(dx, dy))
    for dx in reversed(ring(nx)):
        bx = (x + dx) % nx
        rows = pl.ds(pl.multiple_of(keep_row + bx * x_rows, x_rows), x_rows)
        count = ny - 1 if dx == 0 else ny
        drain(total.at[pl.ds(0, count * piece)], part_recv.at[bx])
        push(total.at[rows], total.at[rows], 7, ar_recv.at[5], partner)
    drain(total.at[pl.ds(0, half_rows)], ar_recv.at[5])
    grad_copy = pltpu.make_async_copy(total, grad_hbm, out_sem.at[1])
    grad_copy.start()

    halo_sent(win0, blocks_dev, 0)
    for turn, win in enumerate(wins):
        halo_sent(win, mesh_dev, turn + 1)
    drain(st0.at[pl.ds(0, 1)], ar_send.at[0])
    drain(grad.at[pl.ds(0, half_rows)], ar_send.at[1])
    drain(st1.at[pl.ds(0, others)], ar_send.at[2])
    drain(s1.at[pl.ds(0, others)], ar_send.at[3])
    drain(st2.at[pl.ds(0, nz - 1)], ar_send.at[4])
    drain(s2.at[pl.ds(0, nz - 1)], ar_send.at[5])
    drain(total.at[pl.ds(0, others * piece)], ar_send.at[6])
    drain(total.at[pl.ds(0, half_rows)], ar_send.at[7])
    pred_copy.wait()
    grad_copy.wait()


def shards(
    nz,
    grid_in,
    target,
    w_enc,
    w_mix_self,
    w_mix_nbr,
    w_dec,
    w_out,
    var_weight,
    g2m_idx,
    g2m_w,
    mesh_nbr,
    m2g_idx,
    m2g_w,
):
    n_lat = lax.axis_size("lat")
    n_lon = lax.axis_size("lon")
    ny = n_lat // nz
    points, width = grid_in.shape
    n_var = target.shape[1]
    mesh_dev = mesh_nbr.shape[0]
    turned = (g2m_idx.T, g2m_w.T, mesh_nbr.T, m2g_idx.T, m2g_w.T)
    blocks_dev = points // BS
    piece = width // (n_lon * ny)
    window = 9 * mesh_dev
    hbm = pl.BlockSpec(memory_space=pl.ANY)
    vmem = pl.BlockSpec(memory_space=pltpu.VMEM)
    pred, loss, grad = pl.pallas_call(
        functools.partial(program_kernel, n_lat, n_lon, nz),
        name="forecast_step",
        out_shape=(
            jax.ShapeDtypeStruct((points, n_var), F32),
            jax.ShapeDtypeStruct((1, n_var), F32),
            jax.ShapeDtypeStruct((width, n_var), F32),
        ),
        in_specs=[hbm] * 7 + [vmem] + [hbm] * 5,
        out_specs=(hbm, vmem, hbm),
        scratch_shapes=[
            pltpu.VMEM((points, width), F32),
            pltpu.VMEM((points, n_var), F32),
            pltpu.VMEM((6, width, width), F32),
            pltpu.VMEM((width, n_var), F32),
            *[pltpu.VMEM(a.shape, a.dtype) for a in turned],
            pltpu.VMEM(m2g_idx.shape, jnp.int32),
            pltpu.VMEM(m2g_w.shape, F32),
            pltpu.VMEM((6, 2, width, width), BF16),
            pltpu.VMEM((2, width, n_var), BF16),
            pltpu.VMEM((2, points, width), BF16),
            pltpu.VMEM((points, width), F32),
            pltpu.VMEM((2, points, window), BF16),
            pltpu.VMEM((9 * blocks_dev, width), F32),
            pltpu.VMEM((window, width), F32),
            pltpu.VMEM((window, width), F32),
            pltpu.VMEM((window, width), F32),
            pltpu.VMEM((points, n_var), F32),
            pltpu.VMEM((width, n_var), F32),
            pltpu.VMEM((width // 2, n_var), F32),
            pltpu.VMEM((width // 2, n_var), F32),
            pltpu.VMEM((n_lon // 2 * ny, piece, n_var), F32),
            pltpu.VMEM((nz, piece, n_var), F32),
            pltpu.VMEM((width, n_var), F32),
            pltpu.VMEM((2, 2, n_var), F32),
            pltpu.VMEM((n_lon // 2 * ny, 2, n_var), F32),
            pltpu.VMEM((nz, 2, n_var), F32),
            pltpu.SemaphoreType.DMA((18,)),
            pltpu.SemaphoreType.DMA((2,)),
            pltpu.SemaphoreType.DMA((4, 3)),
            pltpu.SemaphoreType.DMA((4,)),
            pltpu.SemaphoreType.DMA((n_lon // 2,)),
            pltpu.SemaphoreType.DMA((n_lon // 2,)),
            pltpu.SemaphoreType.DMA((6,)),
            pltpu.SemaphoreType.DMA((8,)),
        ],
        compiler_params=pltpu.CompilerParams(collective_id=0, has_side_effects=True),
    )(
        grid_in,
        target,
        w_enc,
        w_mix_self,
        w_mix_nbr,
        w_dec,
        w_out,
        var_weight.reshape(1, n_var),
        *turned,
    )
    return (pred, loss[0, 0], grad)


def solution(mesh, nz=NZ):
    rows = P(("lat", "lon"), None)
    placed = (rows, rows, P(), P(), P(), P(), P(), P(), rows, rows, rows, rows, rows)
    return jax.shard_map(
        functools.partial(shards, nz),
        mesh=mesh,
        in_specs=placed,
        out_specs=(rows, P(), P()),
        check_vma=False,
    )
```

```python
import functools

import jax
import jax.numpy as jnp
from jax import lax
from jax.experimental import pallas as pl
from jax.experimental.pallas import tpu as pltpu
from jax.sharding import PartitionSpec as P

BS = 16
L = 2
NZ = 12
EPS = 1e-05
F32 = jnp.float32
BF16 = jnp.bfloat16
MESH = pl.DeviceIdType.MESH


def split(value):
    high = value.astype(BF16)
    low = (value - high.astype(F32)).astype(BF16)
    return high, low


def dot(left, right):
    return jnp.dot(left, right, preferred_element_type=F32)


def mm3(left, right):
    (lh, ll), (rh, rl) = left, right
    rows = lh.shape[0]
    both = dot(jnp.concatenate([lh, ll], axis=0), rh)
    return both[:rows] + (both[rows:] + dot(lh, rl))


def silu(value):
    return value / (1.0 + jnp.exp(-value))


def span(index, size):
    return pl.ds(pl.multiple_of(index * size, size), size)


def lanes(count):
    return -(-count // 128) * 128


def program_kernel(
    n_lat,
    n_lon,
    nz,
    grid_hbm,
    target_hbm,
    w_enc_hbm,
    w_self_hbm,
    w_nbr_hbm,
    w_dec_hbm,
    w_out_hbm,
    vw_hbm,
    g_idx_hbm,
    g_w_hbm,
    nbr_hbm,
    m_idx_hbm,
    m_w_hbm,
    pred_out,
    loss_out,
    grad_out,
    grid,
    target,
    w_f32,
    w_out,
    vw,
    g_idx,
    g_w,
    nbr,
    m_idx,
    m_w,
    m_idx_cols,
    m_w_cols,
    w_bf,
    w_out_bf,
    h_bf,
    h_dec,
    back_bf,
    win0,
    win1,
    win2,
    win3,
    pred,
    grad,
    half,
    s1_src,
    s1,
    s2,
    done,
    loss_row,
    st0,
    st1,
    st2,
    in_sem,
    out_sem,
    halo_recv,
    halo_send,
    half_recv,
    part_recv,
    ar_recv,
    ar_send,
):
    lat = lax.axis_index("lat")
    lon = lax.axis_index("lon")
    ny = n_lat // nz
    y = lat // nz
    z = lat % nz
    points, width = grid.shape
    n_var = target.shape[1]
    piece = s2.shape[1]
    nx = n_lon // 2
    x = lon // 2
    core = lon % 2
    x_rows = ny * piece
    half_rows = nx * x_rows
    grid_total = float(points * n_lat * n_lon)

    inner = 1 - 2 * core
    outer = -inner

    def near(lat_step, lon_step):
        return ((lat + lat_step + n_lat) % n_lat, (lon + lon_step + n_lon) % n_lon)

    def at_xy(dx, dy):
        return (((y + dy) % ny) * nz + z, ((x + dx) % nx) * 2 + core)

    def at_z(step):
        return (y * nz + (z + step) % nz, lon)

    def ring(count):
        return sorted(range(count), key=lambda d: (-min(d, count - d), d))

    xy_order = [(dx, dy) for dx in range(nx) for dy in range(ny) if dx or dy]
    xy_order.sort(key=lambda d: -(min(d[0], nx - d[0]) + min(d[1], ny - d[1])))
    z_order = [d for d in ring(nz) if d]

    peers = [near(1, 0), near(-1, 0), near(1, outer), near(-1, outer), near(0, outer), near(0, inner)]
    peers += [at_xy(dx, dy) for dx, dy in xy_order]
    peers += [at_z(d) for d in z_order]

    barrier = pltpu.get_barrier_semaphore()
    for peer in peers:
        pl.semaphore_signal(barrier, inc=1, device_id=peer, device_id_type=MESH)

    def load(source, dest, slot):
        return pltpu.make_async_copy(source, dest, in_sem.at[slot])

    quarter = width // 4
    first = [
        load(w_enc_hbm.at[pl.ds(q * quarter, quarter)], w_f32.at[0, pl.ds(q * quarter, quarter)], q)
        for q in range(4)
    ]
    first += [
        load(grid_hbm.at[pl.ds(q * 128, 128)], grid.at[pl.ds(q * 128, 128)], 4 + q)
        for q in range(points // 128)
    ]
    later = [
        load(nbr_hbm, nbr, 6),
        load(m_idx_hbm, m_idx, 7),
        load(m_w_hbm, m_w, 8),
        load(w_dec_hbm, w_f32.at[1], 9),
        load(w_self_hbm.at[0], w_f32.at[2], 10),
        load(w_nbr_hbm.at[0], w_f32.at[3], 11),
        load(w_self_hbm.at[1], w_f32.at[4], 12),
        load(w_nbr_hbm.at[1], w_f32.at[5], 13),
        load(w_out_hbm, w_out, 14),
        load(target_hbm, target, 15),
        load(g_idx_hbm, g_idx, 16),
        load(g_w_hbm, g_w, 17),
        load(vw_hbm, vw, 18),
    ]
    for copy in first:
        copy.start()

    def split_weight(which, start=0, count=8):
        def body(step, carry):
            rows = span(step, width // 8)
            high, low = split(w_f32[which, rows, :])
            w_bf[which, 0, rows, :] = high
            w_bf[which, 1, rows, :] = low
            return carry

        lax.fori_loop(start, start + count, body, 0)

    def weight(which):
        return w_bf[which, 0], w_bf[which, 1]

    def locate(index, rows):
        shift = rows.bit_length() - 1
        lon_shift = n_lon.bit_length() - 1
        owner = index >> shift
        within = index & (rows - 1)
        band_slot = (owner >> lon_shift) - lat + 1
        tile_slot = ((owner & (n_lon - 1)) - lon + 1 + n_lon) & (n_lon - 1)
        lone = jnp.where(tile_slot == 1, 0, 1 + (tile_slot >> 1))
        other = jnp.where(tile_slot == 1, 3 + (band_slot >> 1), (band_slot & 2) + (tile_slot >> 1))
        far = jnp.where((band_slot == 1) | (tile_slot == 1), 0, lanes(5 * rows))
        return (jnp.where(band_slot == 1, lone, other) << shift) + within + far

    def select(local, factors, columns):
        place = lax.broadcasted_iota(jnp.int32, (local.shape[0], columns), 1)
        chosen = jnp.zeros((local.shape[0], columns), F32)
        for k in range(local.shape[1]):
            value = 1.0 if factors is None else factors[:, k : k + 1]
            chosen = chosen + jnp.where(place == local[:, k : k + 1], value, 0.0)
        return chosen

    def send(win, rows, turn, source, dest, group, peer):
        pltpu.make_async_remote_copy(
            src_ref=win.at[span(source, rows)],
            dst_ref=win.at[span(dest, rows)],
            send_sem=halo_send.at[turn],
            recv_sem=halo_recv.at[turn, group],
            device_id=peer,
            device_id_type=MESH,
        ).start()

    def lon_slot(step):
        return 1 + (step + 1) // 2

    def lat_slot(step):
        return 3 + (step + 1) // 2

    def corner(lat_step, lon_step):
        return 5 + (lat_step + 1) + (lon_step + 1) // 2

    def halo_start(win, rows, turn):
        for step in (1, -1):
            send(win, rows, turn, 0, lat_slot(-step), lat_slot(-step) - 2, near(step, 0))
        for step in (1, -1):
            send(win, rows, turn, 0, corner(-step, -outer), 3, near(step, outer))
        send(win, rows, turn, 0, lon_slot(-outer), 0, near(0, outer))
        send(win, rows, turn, 0, lon_slot(-inner), 0, near(0, inner))

    def halo_wait(win, rows, turn, group, count):
        part = win.at[pl.ds(0, count * rows)]
        pltpu.make_async_copy(part, part, halo_recv.at[turn, group]).wait()

    def halo_forward(win, rows, turn):
        for step in (-1, 1):
            halo_wait(win, rows, turn, lat_slot(step) - 2, 1)
            send(win, rows, turn, lat_slot(step), corner(step, -inner), 3, near(0, inner))

    def halo_inner(win, rows, turn):
        halo_wait(win, rows, turn, 0, 2)
        return split(win[0 : 5 * rows, :])

    def halo_corners(win, rows, turn):
        halo_wait(win, rows, turn, 3, 4)
        return split(win[5 * rows : 9 * rows, :])

    def columns(parts, start, stop):
        return tuple(part[:, start:stop] for part in parts)

    def halo_sent(win, rows, turn):
        part = win.at[pl.ds(0, 8 * rows)]
        pltpu.make_async_copy(part, part, halo_send.at[turn]).wait()

    blocks_dev = points // BS
    mesh_dev = nbr.shape[1]
    for q in range(4):
        first[q].wait()
        split_weight(0, 2 * q, 2)
    for copy in later:
        copy.start()
    for copy in first[4:]:
        copy.wait()

    def encode(step, carry):
        rows = span(step, 128)
        value = grid[rows, :]
        h_one = value + silu(mm3(split(value), weight(0)))
        high, low = split(h_one)
        h_bf[0, rows, :] = high
        h_bf[1, rows, :] = low
        means = jnp.sum(h_one.reshape(128 // BS, BS, width), axis=1) * (1.0 / BS)
        start = pl.multiple_of(step * (128 // BS), 128 // BS)
        win0[pl.ds(start, 128 // BS), :] = means
        return carry

    lax.fori_loop(0, points // 128, encode, 0)
    pl.semaphore_wait(barrier, len(peers))
    halo_start(win0, blocks_dev, 0)

    later[10].wait()
    later[11].wait()
    g_weights = g_w[...].T
    g_local = locate(g_idx[...].T, blocks_dev)
    g_far = lanes(5 * blocks_dev)
    g_select = split(select(g_local, g_weights, g_far + 4 * blocks_dev))
    g_total = jnp.sum(g_weights, axis=1, keepdims=True)
    later[0].wait()
    far = lanes(5 * mesh_dev)
    a_select = select(locate(nbr[...].T, mesh_dev), None, far + 4 * mesh_dev).astype(BF16)
    later[4].wait()
    split_weight(2)
    later[5].wait()
    split_weight(3)
    halo_forward(win0, blocks_dev, 0)
    cut = 5 * blocks_dev
    mesh = mm3(columns(g_select, 0, cut), halo_inner(win0, blocks_dev, 0))
    mesh = mesh + mm3(columns(g_select, g_far, g_far + 4 * blocks_dev), halo_corners(win0, blocks_dev, 0))
    mesh = mesh / g_total

    def hidden_part(step, carry):
        rows = span(step, 128)
        h_dec[rows, :] = mm3((h_bf[0, rows, :], h_bf[1, rows, :]), weight(1))
        return carry

    def gather(parts):
        high, low = parts[1]
        return dot(parts[0], high) + dot(parts[0], low)

    cut = 5 * mesh_dev
    wins = (win1, win2, win3)

    def own(win):
        return pl.ds(0, mesh_dev)

    for layer in range(L):
        win = wins[layer]
        win[own(win), :] = mesh
        halo_start(win, mesh_dev, layer + 1)
        center = mesh - jnp.mean(mesh, axis=1, keepdims=True)
        spread = jnp.mean(center * center, axis=1, keepdims=True)
        nrm = center / jnp.sqrt(spread + EPS)
        self_part = mm3(split(nrm), weight(2 + 2 * layer))
        if layer == 0:
            for ready, which in ((6, 4), (7, 5)):
                later[ready].wait()
                split_weight(which)
            later[3].wait()
            split_weight(1)
            halo_forward(win, mesh_dev, layer + 1)
            later[1].wait()
            later[2].wait()
            factors = m_w[...].T
            m_w_cols[...] = factors / jnp.sum(factors, axis=1, keepdims=True)
            m_idx_cols[...] = locate(m_idx[...].T, mesh_dev)

            def build(step, carry):
                rows = span(step, 64)
                chosen = select(m_idx_cols[rows, :], m_w_cols[rows, :], far + 4 * mesh_dev)
                high, low = split(chosen)
                back_bf[0, rows, :] = high
                back_bf[1, rows, :] = low
                return carry

            lax.fori_loop(0, points // 64, build, 0)
        else:
            lax.fori_loop(0, points // 128, hidden_part, 0)
            halo_forward(win, mesh_dev, layer + 1)
        agg = gather((a_select[:, :cut], halo_inner(win, mesh_dev, layer + 1)))
        agg = agg + gather((a_select[:, far:], halo_corners(win, mesh_dev, layer + 1)))
        agg = agg / float(nbr.shape[0])
        mesh = mesh + silu(self_part + mm3(split(agg), weight(3 + 2 * layer)))

    win3[own(win3), :] = mm3(split(mesh), weight(1))
    halo_start(win3, mesh_dev, 3)
    later[8].wait()
    high, low = split(w_out[...])
    w_out_bf[0] = high
    w_out_bf[1] = low
    halo_forward(win3, mesh_dev, 3)
    later[9].wait()
    power = jnp.sum(target[...] * target[...], axis=0, keepdims=True)
    later[12].wait()
    weights = vw[...].astype(F32)
    wsum = jnp.sum(weights, axis=1, keepdims=True)
    table = halo_inner(win3, mesh_dev, 3)
    for step in range(points // 128):
        rows = pl.ds(step * 128, 128)
        h_dec[rows, :] += mm3((back_bf[0, rows, 0:cut], back_bf[1, rows, 0:cut]), table)
    table = halo_corners(win3, mesh_dev, 3)
    w_out_parts = (w_out_bf[0], w_out_bf[1])
    err = jnp.zeros((1, n_var), F32)
    for step in range(points // 128):
        rows = pl.ds(step * 128, 128)
        corners = (back_bf[0, rows, pl.ds(far, 4 * mesh_dev)], back_bf[1, rows, pl.ds(far, 4 * mesh_dev)])
        hidden = silu(h_dec[rows, :] + mm3(corners, table))
        hh, hl = split(hidden)
        out = mm3((hh, hl), w_out_parts)
        pred[rows, :] = out
        resid = out - target[rows, :]
        err = err + jnp.sum(resid * resid, axis=0, keepdims=True)
        part = mm3((hh.T, hl.T), split(resid))
        if step == 0:
            grad[...] = part
        else:
            grad[...] += part
    pred_copy = pltpu.make_async_copy(pred, pred_out, out_sem.at[0])
    pred_copy.start()

    def push(source, dest, stage, recv, peer):
        pltpu.make_async_remote_copy(
            src_ref=source,
            dst_ref=dest,
            send_sem=ar_send.at[stage],
            recv_sem=recv,
            device_id=peer,
            device_id_type=MESH,
        ).start()

    def drain(part, sem):
        pltpu.make_async_copy(part, part, sem).wait()

    partner = near(0, inner)
    me = x * ny + y
    keep_row = core * half_rows

    st0[core] = jnp.concatenate([power, err], axis=0)
    push(st0.at[core], st0.at[core], 0, ar_recv.at[0], partner)
    for dx in ring(nx):
        bx = (x + dx) % nx
        rows = pl.ds(pl.multiple_of((1 - core) * half_rows + bx * x_rows, x_rows), x_rows)
        push(grad.at[rows], half.at[span(bx, x_rows)], 1, half_recv.at[bx], partner)

    drain(st0.at[pl.ds(0, 1)], ar_recv.at[0])
    st1[me] = st0[0] + st0[1]
    for dx, dy in xy_order:
        push(st1.at[me], st1.at[me], 2, ar_recv.at[1], at_xy(dx, dy))
    for dx in ring(nx):
        bx = (x + dx) % nx
        drain(half.at[span(bx, x_rows)], half_recv.at[bx])
        rows = pl.ds(pl.multiple_of(keep_row + bx * x_rows, x_rows), x_rows)
        s1_src[span(bx, x_rows), :] = grad[rows, :] + half[span(bx, x_rows), :]
        for dy in ring(ny):
            if dx or dy:
                block = bx * ny + (y + dy) % ny
                push(s1_src.at[span(block, piece)], s1.at[me], 3, ar_recv.at[2], at_xy(dx, dy))
    s1[me] = s1_src[span(me, piece), :]

    others = nx * ny - 1
    drain(st1.at[pl.ds(0, others)], ar_recv.at[1])
    st2[z] = jnp.sum(st1[...], axis=0)
    for d in z_order:
        push(st2.at[z], st2.at[z], 4, ar_recv.at[3], at_z(d))
    drain(s1.at[pl.ds(0, others)], ar_recv.at[2])
    s2[z] = jnp.sum(s1[...], axis=0)
    for d in z_order:
        push(s2.at[z], s2.at[z], 5, ar_recv.at[4], at_z(d))

    drain(st2.at[pl.ds(0, nz - 1)], ar_recv.at[3])
    stats = jnp.sum(st2[...], axis=0)
    scale = stats[0:1] / grid_total + 1e-06
    norm = scale * grid_total * wsum
    loss = jnp.sum(weights * stats[1:2] / norm, axis=1, keepdims=True)
    loss_row[...] = jnp.broadcast_to(loss, loss_row.shape)
    loss_copy = pltpu.make_async_copy(loss_row, loss_out, out_sem.at[1])
    loss_copy.start()
    coef = 2.0 * weights / norm

    drain(s2.at[pl.ds(0, nz - 1)], ar_recv.at[4])
    mine = pl.ds(pl.multiple_of(keep_row + me * piece, piece), piece)
    done[...] = jnp.sum(s2[...], axis=0) * coef
    for dx, dy in xy_order:
        push(done, grad_out.at[mine], 6, part_recv.at[x], at_xy(dx, dy))
    done_copy = pltpu.make_async_copy(done, grad_out.at[mine], out_sem.at[2])
    done_copy.start()
    done_copy.wait()
    for dx in reversed(ring(nx)):
        bx = (x + dx) % nx
        rows = pl.ds(pl.multiple_of(keep_row + bx * x_rows, x_rows), x_rows)
        count = ny - 1 if dx == 0 else ny
        drain(grad_out.at[pl.ds(0, count * piece)], part_recv.at[bx])
        push(grad_out.at[rows], grad_out.at[rows], 7, ar_recv.at[5], partner)
    drain(grad_out.at[pl.ds(0, half_rows)], ar_recv.at[5])

    halo_sent(win0, blocks_dev, 0)
    for turn, win in enumerate(wins):
        halo_sent(win, mesh_dev, turn + 1)
    drain(st0.at[pl.ds(0, 1)], ar_send.at[0])
    drain(grad.at[pl.ds(0, half_rows)], ar_send.at[1])
    drain(st1.at[pl.ds(0, others)], ar_send.at[2])
    drain(s1.at[pl.ds(0, others)], ar_send.at[3])
    drain(st2.at[pl.ds(0, nz - 1)], ar_send.at[4])
    drain(s2.at[pl.ds(0, nz - 1)], ar_send.at[5])
    drain(s1.at[pl.ds(0, others)], ar_send.at[6])
    drain(grad_out.at[pl.ds(0, half_rows)], ar_send.at[7])
    pred_copy.wait()
    loss_copy.wait()


def shards(
    nz,
    grid_in,
    target,
    w_enc,
    w_mix_self,
    w_mix_nbr,
    w_dec,
    w_out,
    var_weight,
    g2m_idx,
    g2m_w,
    mesh_nbr,
    m2g_idx,
    m2g_w,
):
    n_lat = lax.axis_size("lat")
    n_lon = lax.axis_size("lon")
    ny = n_lat // nz
    points, width = grid_in.shape
    n_var = target.shape[1]
    mesh_dev = mesh_nbr.shape[0]
    turned = (g2m_idx.T, g2m_w.T, mesh_nbr.T, m2g_idx.T, m2g_w.T)
    blocks_dev = points // BS
    piece = width // (n_lon * ny)
    window = 9 * mesh_dev
    vw = var_weight.reshape(1, n_var)
    operands = (grid_in, target, w_enc, w_mix_self, w_mix_nbr, w_dec, w_out, vw, *turned)
    hbm = pl.BlockSpec(memory_space=pl.ANY)
    pred, loss, grad = pl.pallas_call(
        functools.partial(program_kernel, n_lat, n_lon, nz),
        name="forecast_step",
        out_shape=(
            jax.ShapeDtypeStruct((points, n_var), F32),
            jax.ShapeDtypeStruct((1, n_var), F32),
            jax.ShapeDtypeStruct((width, n_var), F32),
        ),
        in_specs=[hbm] * len(operands),
        out_specs=(hbm, hbm, hbm),
        scratch_shapes=[
            pltpu.VMEM((points, width), F32),
            pltpu.VMEM((points, n_var), F32),
            pltpu.VMEM((6, width, width), F32),
            pltpu.VMEM((width, n_var), F32),
            pltpu.VMEM((1, n_var), jnp.int32),
            *[pltpu.VMEM(a.shape, a.dtype) for a in turned],
            pltpu.VMEM(m2g_idx.shape, jnp.int32),
            pltpu.VMEM(m2g_w.shape, F32),
            pltpu.VMEM((6, 2, width, width), BF16),
            pltpu.VMEM((2, width, n_var), BF16),
            pltpu.VMEM((2, points, width), BF16),
            pltpu.VMEM((points, width), F32),
            pltpu.VMEM((2, points, lanes(5 * mesh_dev) + 4 * mesh_dev), BF16),
            pltpu.VMEM((9 * blocks_dev, width), F32),
            pltpu.VMEM((window, width), F32),
            pltpu.VMEM((window, width), F32),
            pltpu.VMEM((window, width), F32),
            pltpu.VMEM((points, n_var), F32),
            pltpu.VMEM((width, n_var), F32),
            pltpu.VMEM((width // 2, n_var), F32),
            pltpu.VMEM((width // 2, n_var), F32),
            pltpu.VMEM((n_lon // 2 * ny, piece, n_var), F32),
            pltpu.VMEM((nz, piece, n_var), F32),
            pltpu.VMEM((piece, n_var), F32),
            pltpu.VMEM((1, n_var), F32),
            pltpu.VMEM((2, 2, n_var), F32),
            pltpu.VMEM((n_lon // 2 * ny, 2, n_var), F32),
            pltpu.VMEM((nz, 2, n_var), F32),
            pltpu.SemaphoreType.DMA((19,)),
            pltpu.SemaphoreType.DMA((3,)),
            pltpu.SemaphoreType.DMA((4, 4)),
            pltpu.SemaphoreType.DMA((4,)),
            pltpu.SemaphoreType.DMA((n_lon // 2,)),
            pltpu.SemaphoreType.DMA((n_lon // 2,)),
            pltpu.SemaphoreType.DMA((6,)),
            pltpu.SemaphoreType.DMA((8,)),
        ],
        compiler_params=pltpu.CompilerParams(
            collective_id=0, has_side_effects=True, vmem_limit_bytes=28 << 20
        ),
    )(*[pltpu.with_memory_space_constraint(a, pltpu.HBM) for a in operands])
    return (pred, loss[0, 0], grad)


def solution(mesh, nz=NZ):
    rows = P(("lat", "lon"), None)
    placed = (rows, rows, P(), P(), P(), P(), P(), P(), rows, rows, rows, rows, rows)
    return jax.shard_map(
        functools.partial(shards, nz),
        mesh=mesh,
        in_specs=placed,
        out_specs=(rows, P(), P()),
        check_vma=False,
    )
```

```python
import functools

import jax
import jax.numpy as jnp
from jax import lax
from jax.experimental import pallas as pl
from jax.experimental.pallas import tpu as pltpu
from jax.sharding import PartitionSpec as P

BS = 16
L = 2
NZ = 12
EPS = 1e-05
F32 = jnp.float32
BF16 = jnp.bfloat16
MESH = pl.DeviceIdType.MESH


def split(value):
    high = value.astype(BF16)
    low = (value - high.astype(F32)).astype(BF16)
    return high, low


def dot(left, right):
    return jnp.dot(left, right, preferred_element_type=F32)


def mm3(left, right):
    (lh, ll), (rh, rl) = left, right
    rows = lh.shape[0]
    both = dot(jnp.concatenate([lh, ll], axis=0), rh)
    return both[:rows] + (both[rows:] + dot(lh, rl))


def silu(value):
    return value / (1.0 + jnp.exp(-value))


def span(index, size):
    return pl.ds(pl.multiple_of(index * size, size), size)


def lanes(count):
    return -(-count // 128) * 128


def place_kernel(pred_in, grad_in, pred_out, grad_out, sem):
    copies = [
        pltpu.make_async_copy(grad_in, grad_out, sem.at[0]),
        pltpu.make_async_copy(pred_in, pred_out, sem.at[1]),
    ]
    for copy in copies:
        copy.start()
    for copy in copies:
        copy.wait()


def program_kernel(
    n_lat,
    n_lon,
    nz,
    grid_hbm,
    target_hbm,
    w_enc_hbm,
    w_self_hbm,
    w_nbr_hbm,
    w_dec_hbm,
    w_out_hbm,
    vw_hbm,
    g_idx_hbm,
    g_w_hbm,
    nbr_hbm,
    m_idx_hbm,
    m_w_hbm,
    pred_out,
    loss_out,
    grad_out,
    grid,
    target,
    w_f32,
    w_out,
    vw,
    g_idx,
    g_w,
    nbr,
    m_idx,
    m_w,
    m_idx_cols,
    m_w_cols,
    w_bf,
    w_out_bf,
    h_bf,
    resid_bf,
    h_dec,
    back_bf,
    win0,
    win1,
    win2,
    win3,
    pred,
    grad,
    half,
    s1_src,
    s1,
    s2,
    done,
    loss_row,
    st0,
    in_sem,
    out_sem,
    halo_recv,
    halo_send,
    half_recv,
    part_recv,
    ar_recv,
    ar_send,
):
    lat = lax.axis_index("lat")
    lon = lax.axis_index("lon")
    ny = n_lat // nz
    y = lat // nz
    z = lat % nz
    points, width = grid.shape
    n_var = target.shape[1]
    piece = done.shape[0]
    nx = n_lon // 2
    x = lon // 2
    core = lon % 2
    x_rows = ny * piece
    half_rows = nx * x_rows
    grid_total = float(points * n_lat * n_lon)

    inner = 1 - 2 * core
    outer = -inner

    def wrap(value, count):
        value = jnp.where(value >= count, value - count, value)
        return jnp.where(value < 0, value + count, value)

    lats = {step: wrap(lat + step, n_lat) for step in (-1, 0, 1)}
    xs = [wrap(x + step, nx) for step in range(nx)]
    ys = [wrap(y + step, ny) for step in range(ny)]
    y_lats = [value * nz + z for value in ys]
    x_lons = [value * 2 + core for value in xs]
    z_lats = [y * nz + wrap(z + step, nz) for step in range(nz)]
    inner_lon = lon + inner
    outer_lon = wrap(lon + outer, n_lon)

    def near(lat_step, to_lon):
        return (lats[lat_step], to_lon)

    def at_xy(dx, dy):
        return (y_lats[dy], x_lons[dx])

    def at_z(step):
        return (z_lats[step], lon)

    def ring(count):
        return sorted(range(count), key=lambda d: (-min(d, count - d), d))

    xy_order = [(dx, dy) for dx in range(nx) for dy in range(ny) if dx or dy]
    xy_order.sort(key=lambda d: -(min(d[0], nx - d[0]) + min(d[1], ny - d[1])))
    z_order = [d for d in ring(nz) if d]

    peers = [near(step, to) for step in (1, -1) for to in (lon, outer_lon)]
    peers += [near(0, outer_lon), near(0, inner_lon)]
    peers += [at_xy(dx, dy) for dx, dy in xy_order]
    peers += [at_z(d) for d in z_order]

    def load(source, dest, slot):
        return pltpu.make_async_copy(source, dest, in_sem.at[slot])

    quarter = width // 4
    first = [
        load(w_enc_hbm.at[pl.ds(q * quarter, quarter)], w_f32.at[0, pl.ds(q * quarter, quarter)], q)
        for q in range(4)
    ]
    first += [
        load(grid_hbm.at[pl.ds(q * 128, 128)], grid.at[pl.ds(q * 128, 128)], 4 + q)
        for q in range(points // 128)
    ]
    later = [
        load(nbr_hbm, nbr, 6),
        load(m_idx_hbm, m_idx, 7),
        load(m_w_hbm, m_w, 8),
        load(w_dec_hbm, w_f32.at[1], 9),
        load(w_self_hbm.at[0], w_f32.at[2], 10),
        load(w_nbr_hbm.at[0], w_f32.at[3], 11),
        load(w_self_hbm.at[1], w_f32.at[4], 12),
        load(w_nbr_hbm.at[1], w_f32.at[5], 13),
        load(w_out_hbm, w_out, 14),
        load(target_hbm, target, 15),
        load(g_idx_hbm, g_idx, 16),
        load(g_w_hbm, g_w, 17),
        load(vw_hbm, vw, 18),
    ]
    for copy in first:
        copy.start()

    barrier = pltpu.get_barrier_semaphore()
    for peer in peers:
        pl.semaphore_signal(barrier, inc=1, device_id=peer, device_id_type=MESH)

    def split_weight(which, start=0, count=8):
        def body(step, carry):
            rows = span(step, width // 8)
            high, low = split(w_f32[which, rows, :])
            w_bf[which, 0, rows, :] = high
            w_bf[which, 1, rows, :] = low
            return carry

        lax.fori_loop(start, start + count, body, 0)

    def weight(which):
        return w_bf[which, 0], w_bf[which, 1]

    def locate(index, rows):
        shift = rows.bit_length() - 1
        lon_shift = n_lon.bit_length() - 1
        owner = index >> shift
        within = index & (rows - 1)
        band_slot = (owner >> lon_shift) - lat + 1
        tile_slot = ((owner & (n_lon - 1)) - lon + 1 + n_lon) & (n_lon - 1)
        lone = jnp.where(tile_slot == 1, 0, 1 + (tile_slot >> 1))
        other = jnp.where(tile_slot == 1, 3 + (band_slot >> 1), (band_slot & 2) + (tile_slot >> 1))
        far = jnp.where((band_slot == 1) | (tile_slot == 1), 0, lanes(5 * rows))
        return (jnp.where(band_slot == 1, lone, other) << shift) + within + far

    def select(local, factors, columns):
        place = lax.broadcasted_iota(jnp.int32, (local.shape[0], columns), 1)
        chosen = jnp.zeros((local.shape[0], columns), F32)
        for k in range(local.shape[1]):
            value = 1.0 if factors is None else factors[:, k : k + 1]
            chosen = chosen + jnp.where(place == local[:, k : k + 1], value, 0.0)
        return chosen

    def send(win, rows, turn, source, dest, group, peer):
        pltpu.make_async_remote_copy(
            src_ref=win.at[span(source, rows)],
            dst_ref=win.at[span(dest, rows)],
            send_sem=halo_send.at[turn],
            recv_sem=halo_recv.at[turn, group],
            device_id=peer,
            device_id_type=MESH,
        ).start()

    def lon_slot(step):
        return 1 + (step + 1) // 2

    def lat_slot(step):
        return 3 + (step + 1) // 2

    def corner(lat_step, lon_step):
        return 5 + (lat_step + 1) + (lon_step + 1) // 2

    def halo_start(win, rows, turn):
        for step in (1, -1):
            send(win, rows, turn, 0, lat_slot(-step), lat_slot(-step) - 2, near(step, lon))
        for step in (1, -1):
            send(win, rows, turn, 0, corner(-step, -outer), 3, near(step, outer_lon))
        send(win, rows, turn, 0, lon_slot(-outer), 0, near(0, outer_lon))
        send(win, rows, turn, 0, lon_slot(-inner), 0, near(0, inner_lon))

    def halo_wait(win, rows, turn, group, count):
        part = win.at[pl.ds(0, count * rows)]
        pltpu.make_async_copy(part, part, halo_recv.at[turn, group]).wait()

    def halo_forward(win, rows, turn):
        for step in (-1, 1):
            halo_wait(win, rows, turn, lat_slot(step) - 2, 1)
            send(win, rows, turn, lat_slot(step), corner(step, -inner), 3, near(0, inner_lon))

    def halo_inner(win, rows, turn):
        halo_wait(win, rows, turn, 0, 2)
        return split(win[0 : 5 * rows, :])

    def halo_corners(win, rows, turn):
        halo_wait(win, rows, turn, 3, 4)
        return split(win[5 * rows : 9 * rows, :])

    def columns(parts, start, stop):
        return tuple(part[:, start:stop] for part in parts)

    def halo_sent(win, rows, turn):
        part = win.at[pl.ds(0, 8 * rows)]
        pltpu.make_async_copy(part, part, halo_send.at[turn]).wait()

    blocks_dev = points // BS
    mesh_dev = nbr.shape[1]
    for q in range(4):
        first[q].wait()
        split_weight(0, 2 * q, 2)
    for copy in later:
        copy.start()
    for copy in first[4:]:
        copy.wait()

    def encode(step, carry):
        rows = span(step, 128)
        value = grid[rows, :]
        h_one = value + silu(mm3(split(value), weight(0)))
        high, low = split(h_one)
        h_bf[0, rows, :] = high
        h_bf[1, rows, :] = low
        means = jnp.sum(h_one.reshape(128 // BS, BS, width), axis=1) * (1.0 / BS)
        start = pl.multiple_of(step * (128 // BS), 128 // BS)
        win0[pl.ds(start, 128 // BS), :] = means
        return carry

    lax.fori_loop(0, points // 128, encode, 0)
    pl.semaphore_wait(barrier, len(peers))
    halo_start(win0, blocks_dev, 0)

    later[10].wait()
    later[11].wait()
    g_weights = g_w[...].T
    g_local = locate(g_idx[...].T, blocks_dev)
    g_far = lanes(5 * blocks_dev)
    g_select = split(select(g_local, g_weights, g_far + 4 * blocks_dev))
    g_total = jnp.sum(g_weights, axis=1, keepdims=True)
    later[0].wait()
    far = lanes(5 * mesh_dev)
    a_select = select(locate(nbr[...].T, mesh_dev), None, far + 4 * mesh_dev).astype(BF16)
    later[4].wait()
    split_weight(2)
    later[5].wait()
    split_weight(3)
    halo_forward(win0, blocks_dev, 0)
    cut = 5 * blocks_dev
    mesh = mm3(columns(g_select, 0, cut), halo_inner(win0, blocks_dev, 0))
    mesh = mesh + mm3(columns(g_select, g_far, g_far + 4 * blocks_dev), halo_corners(win0, blocks_dev, 0))
    mesh = mesh / g_total

    def hidden_part(step, carry):
        rows = span(step, 128)
        h_dec[rows, :] = mm3((h_bf[0, rows, :], h_bf[1, rows, :]), weight(1))
        return carry

    def gather(parts):
        high, low = parts[1]
        return dot(parts[0], high) + dot(parts[0], low)

    cut = 5 * mesh_dev
    wins = (win1, win2, win3)

    def own(win):
        return pl.ds(0, mesh_dev)

    for layer in range(L):
        win = wins[layer]
        win[own(win), :] = mesh
        halo_start(win, mesh_dev, layer + 1)
        center = mesh - jnp.mean(mesh, axis=1, keepdims=True)
        spread = jnp.mean(center * center, axis=1, keepdims=True)
        nrm = center / jnp.sqrt(spread + EPS)
        self_part = mm3(split(nrm), weight(2 + 2 * layer))
        if layer == 0:
            for ready, which in ((6, 4), (7, 5)):
                later[ready].wait()
                split_weight(which)
            later[3].wait()
            split_weight(1)
            halo_forward(win, mesh_dev, layer + 1)
            later[1].wait()
            later[2].wait()
            factors = m_w[...].T
            m_w_cols[...] = factors / jnp.sum(factors, axis=1, keepdims=True)
            m_idx_cols[...] = locate(m_idx[...].T, mesh_dev)

            def build(step, carry):
                rows = span(step, 64)
                chosen = select(m_idx_cols[rows, :], m_w_cols[rows, :], far + 4 * mesh_dev)
                high, low = split(chosen)
                back_bf[0, rows, :] = high
                back_bf[1, rows, :] = low
                return carry

            lax.fori_loop(0, points // 64, build, 0)
        else:
            lax.fori_loop(0, points // 128, hidden_part, 0)
            halo_forward(win, mesh_dev, layer + 1)
        agg = gather((a_select[:, :cut], halo_inner(win, mesh_dev, layer + 1)))
        agg = agg + gather((a_select[:, far:], halo_corners(win, mesh_dev, layer + 1)))
        agg = agg / float(nbr.shape[0])
        mesh = mesh + silu(self_part + mm3(split(agg), weight(3 + 2 * layer)))

    win3[own(win3), :] = mm3(split(mesh), weight(1))
    halo_start(win3, mesh_dev, 3)
    later[8].wait()
    high, low = split(w_out[...])
    w_out_bf[0] = high
    w_out_bf[1] = low
    halo_forward(win3, mesh_dev, 3)
    later[9].wait()
    power = jnp.sum(target[...] * target[...], axis=0, keepdims=True)
    later[12].wait()
    weights = vw[...].astype(F32)
    wsum = jnp.sum(weights, axis=1, keepdims=True)
    table = halo_inner(win3, mesh_dev, 3)
    for step in range(points // 128):
        rows = pl.ds(step * 128, 128)
        h_dec[rows, :] += mm3((back_bf[0, rows, 0:cut], back_bf[1, rows, 0:cut]), table)
    table = halo_corners(win3, mesh_dev, 3)
    w_out_parts = (w_out_bf[0], w_out_bf[1])
    err = jnp.zeros((1, n_var), F32)
    for step in range(points // 128):
        rows = pl.ds(step * 128, 128)
        corners = (back_bf[0, rows, pl.ds(far, 4 * mesh_dev)], back_bf[1, rows, pl.ds(far, 4 * mesh_dev)])
        hidden = silu(h_dec[rows, :] + mm3(corners, table))
        hh, hl = split(hidden)
        out = mm3((hh, hl), w_out_parts)
        pred[rows, :] = out
        resid = out - target[rows, :]
        err = err + jnp.sum(resid * resid, axis=0, keepdims=True)
        h_bf[0, rows, :] = hh
        h_bf[1, rows, :] = hl
        high, low = split(resid)
        resid_bf[0, rows, :] = high
        resid_bf[1, rows, :] = low

    def grad_half(start):
        rows = pl.ds(pl.multiple_of(start, half_rows), half_rows)
        left = (h_bf[0, :, rows].T, h_bf[1, :, rows].T)
        grad[rows, :] = mm3(left, (resid_bf[0], resid_bf[1]))
        return rows

    def push(source, dest, stage, recv, peer):
        pltpu.make_async_remote_copy(
            src_ref=source,
            dst_ref=dest,
            send_sem=ar_send.at[stage],
            recv_sem=recv,
            device_id=peer,
            device_id_type=MESH,
        ).start()

    def drain(part, sem):
        pltpu.make_async_copy(part, part, sem).wait()

    partner = near(0, inner_lon)
    me = x * ny + y
    keep_row = core * half_rows

    st0[core] = jnp.concatenate([power, err], axis=0)
    push(st0.at[core], st0.at[core], 0, ar_recv.at[0], partner)
    given = grad_half((1 - core) * half_rows)
    push(grad.at[given], half, 1, half_recv.at[0], partner)
    kept = grad_half(keep_row)
    pred_copy = pltpu.make_async_copy(pred, pred_out, out_sem.at[0])
    pred_copy.start()

    drain(st0.at[pl.ds(0, 1)], ar_recv.at[0])
    s1_src[:, piece : piece + 2, :] = jnp.broadcast_to((st0[0] + st0[1])[None], (nx * ny, 2, n_var))
    drain(half, half_recv.at[0])
    s1_src[:, 0:piece, :] = (grad[kept, :] + half[...]).reshape(nx * ny, piece, n_var)
    for dx, dy in xy_order:
        push(s1_src.at[xs[dx] * ny + ys[dy]], s1.at[me], 2, ar_recv.at[1], at_xy(dx, dy))
    s1[me] = s1_src[me]

    others = nx * ny - 1
    drain(s1.at[pl.ds(0, others)], ar_recv.at[1])
    s2[z] = jnp.sum(s1[...], axis=0)
    for d in z_order:
        push(s2.at[z], s2.at[z], 3, ar_recv.at[2], at_z(d))

    drain(s2.at[pl.ds(0, nz - 1)], ar_recv.at[2])
    value = jnp.sum(s2[...], axis=0)
    stats = value[piece : piece + 2]
    scale = stats[0:1] / grid_total + 1e-06
    norm = scale * grid_total * wsum
    coef = 2.0 * weights / norm

    mine = pl.ds(pl.multiple_of(keep_row + me * piece, piece), piece)
    done[...] = value[0:piece] * coef
    for dx, dy in xy_order:
        push(done, grad_out.at[mine], 4, part_recv.at[x], at_xy(dx, dy))
    loss = jnp.sum(weights * stats[1:2] / norm, axis=1, keepdims=True)
    loss_row[...] = jnp.broadcast_to(loss, loss_row.shape)
    loss_copy = pltpu.make_async_copy(loss_row, loss_out, out_sem.at[1])
    loss_copy.start()
    done_copy = pltpu.make_async_copy(done, grad_out.at[mine], out_sem.at[2])
    done_copy.start()
    done_copy.wait()
    for dx in reversed(ring(nx)):
        bx = xs[dx]
        rows = pl.ds(pl.multiple_of(keep_row + bx * x_rows, x_rows), x_rows)
        count = ny - 1 if dx == 0 else ny
        drain(grad_out.at[pl.ds(0, count * piece)], part_recv.at[bx])
        push(grad_out.at[rows], grad_out.at[rows], 5, ar_recv.at[3], partner)
    drain(grad_out.at[pl.ds(0, half_rows)], ar_recv.at[3])

    halo_sent(win0, blocks_dev, 0)
    for turn, win in enumerate(wins):
        halo_sent(win, mesh_dev, turn + 1)
    drain(st0.at[pl.ds(0, 1)], ar_send.at[0])
    drain(grad.at[pl.ds(0, half_rows)], ar_send.at[1])
    drain(s1.at[pl.ds(0, others)], ar_send.at[2])
    drain(s2.at[pl.ds(0, nz - 1)], ar_send.at[3])
    drain(grad_out.at[pl.ds(0, others * piece)], ar_send.at[4])
    drain(grad_out.at[pl.ds(0, half_rows)], ar_send.at[5])
    pred_copy.wait()
    loss_copy.wait()


def shards(
    nz,
    grid_in,
    target,
    w_enc,
    w_mix_self,
    w_mix_nbr,
    w_dec,
    w_out,
    var_weight,
    g2m_idx,
    g2m_w,
    mesh_nbr,
    m2g_idx,
    m2g_w,
):
    n_lat = lax.axis_size("lat")
    n_lon = lax.axis_size("lon")
    ny = n_lat // nz
    points, width = grid_in.shape
    n_var = target.shape[1]
    mesh_dev = mesh_nbr.shape[0]
    turned = (g2m_idx.T, g2m_w.T, mesh_nbr.T, m2g_idx.T, m2g_w.T)
    blocks_dev = points // BS
    piece = width // (n_lon * ny)
    window = 9 * mesh_dev
    vw = var_weight.reshape(1, n_var)
    operands = (grid_in, target, w_enc, w_mix_self, w_mix_nbr, w_dec, w_out, vw, *turned)
    hbm = pl.BlockSpec(memory_space=pl.ANY)
    pred, loss, grad = pl.pallas_call(
        functools.partial(program_kernel, n_lat, n_lon, nz),
        name="forecast_step",
        out_shape=(
            jax.ShapeDtypeStruct((points, n_var), F32),
            jax.ShapeDtypeStruct((1, n_var), F32),
            jax.ShapeDtypeStruct((width, n_var), F32),
        ),
        in_specs=[hbm] * len(operands),
        out_specs=(hbm, hbm, hbm),
        scratch_shapes=[
            pltpu.VMEM((points, width), F32),
            pltpu.VMEM((points, n_var), F32),
            pltpu.VMEM((6, width, width), F32),
            pltpu.VMEM((width, n_var), F32),
            pltpu.VMEM((1, n_var), jnp.int32),
            *[pltpu.VMEM(a.shape, a.dtype) for a in turned],
            pltpu.VMEM(m2g_idx.shape, jnp.int32),
            pltpu.VMEM(m2g_w.shape, F32),
            pltpu.VMEM((6, 2, width, width), BF16),
            pltpu.VMEM((2, width, n_var), BF16),
            pltpu.VMEM((2, points, width), BF16),
            pltpu.VMEM((2, points, n_var), BF16),
            pltpu.VMEM((points, width), F32),
            pltpu.VMEM((2, points, lanes(5 * mesh_dev) + 4 * mesh_dev), BF16),
            pltpu.VMEM((9 * blocks_dev, width), F32),
            pltpu.VMEM((window, width), F32),
            pltpu.VMEM((window, width), F32),
            pltpu.VMEM((window, width), F32),
            pltpu.VMEM((points, n_var), F32),
            pltpu.VMEM((width, n_var), F32),
            pltpu.VMEM((width // 2, n_var), F32),
            pltpu.VMEM((n_lon // 2 * ny, piece + 2, n_var), F32),
            pltpu.VMEM((n_lon // 2 * ny, piece + 2, n_var), F32),
            pltpu.VMEM((nz, piece + 2, n_var), F32),
            pltpu.VMEM((piece, n_var), F32),
            pltpu.VMEM((1, n_var), F32),
            pltpu.VMEM((2, 2, n_var), F32),
            pltpu.SemaphoreType.DMA((19,)),
            pltpu.SemaphoreType.DMA((3,)),
            pltpu.SemaphoreType.DMA((4, 4)),
            pltpu.SemaphoreType.DMA((4,)),
            pltpu.SemaphoreType.DMA((1,)),
            pltpu.SemaphoreType.DMA((n_lon // 2,)),
            pltpu.SemaphoreType.DMA((4,)),
            pltpu.SemaphoreType.DMA((6,)),
        ],
        compiler_params=pltpu.CompilerParams(
            collective_id=0, has_side_effects=True, vmem_limit_bytes=28 << 20
        ),
    )(*[pltpu.with_memory_space_constraint(a, pltpu.HBM) for a in operands])
    pred, grad = pl.pallas_call(
        place_kernel,
        name="place",
        out_shape=(
            jax.ShapeDtypeStruct((points, n_var), F32),
            jax.ShapeDtypeStruct((width, n_var), F32),
        ),
        in_specs=[hbm] * 2,
        out_specs=(hbm, hbm),
        scratch_shapes=[pltpu.SemaphoreType.DMA((2,))],
        compiler_params=pltpu.CompilerParams(vmem_limit_bytes=1 << 20),
    )(pred, grad)
    return (pred, loss[0, 0], grad)


def solution(mesh, nz=NZ):
    rows = P(("lat", "lon"), None)
    placed = (rows, rows, P(), P(), P(), P(), P(), P(), rows, rows, rows, rows, rows)
    return jax.shard_map(
        functools.partial(shards, nz),
        mesh=mesh,
        in_specs=placed,
        out_specs=(rows, P(), P()),
        check_vma=False,
    )
```

```python
import functools

import jax
import jax.numpy as jnp
from jax import lax
from jax.experimental import pallas as pl
from jax.experimental.pallas import tpu as pltpu
from jax.sharding import PartitionSpec as P

BS = 16
L = 2
NZ = 12
EPS = 1e-05
F32 = jnp.float32
BF16 = jnp.bfloat16
MESH = pl.DeviceIdType.MESH


def split(value):
    high = value.astype(BF16)
    low = (value - high.astype(F32)).astype(BF16)
    return high, low


def dot(left, right):
    return jnp.dot(left, right, preferred_element_type=F32)


def mm3(left, right):
    (lh, ll), (rh, rl) = left, right
    rows = lh.shape[0]
    both = dot(jnp.concatenate([lh, ll], axis=0), rh)
    return both[:rows] + (both[rows:] + dot(lh, rl))


def silu(value):
    return value / (1.0 + jnp.exp(-value))


def span(index, size):
    return pl.ds(pl.multiple_of(index * size, size), size)


def lanes(count):
    return -(-count // 128) * 128


def place_kernel(pred_in, grad_in, pred_out, grad_out, sem):
    copies = [
        pltpu.make_async_copy(grad_in, grad_out, sem.at[0]),
        pltpu.make_async_copy(pred_in, pred_out, sem.at[1]),
    ]
    for copy in copies:
        copy.start()
    for copy in copies:
        copy.wait()


def program_kernel(
    n_lat,
    n_lon,
    nz,
    grid_hbm,
    target_hbm,
    w_enc_hbm,
    w_self_hbm,
    w_nbr_hbm,
    w_dec_hbm,
    w_out_hbm,
    vw_hbm,
    g_idx_hbm,
    g_w_hbm,
    nbr_hbm,
    m_idx_hbm,
    m_w_hbm,
    pred_out,
    loss_out,
    grad_out,
    grid,
    target,
    w_f32,
    w_out,
    vw,
    g_idx,
    g_w,
    nbr,
    m_idx,
    m_w,
    m_idx_cols,
    m_w_cols,
    w_bf,
    w_out_bf,
    h_bf,
    resid_bf,
    h_dec,
    back_bf,
    win0,
    win1,
    win2,
    win3,
    pred,
    grad,
    half,
    s1_src,
    s1,
    s2,
    done,
    loss_row,
    st0,
    in_sem,
    out_sem,
    halo_recv,
    halo_send,
    half_recv,
    part_recv,
    ar_recv,
    ar_send,
):
    lat = lax.axis_index("lat")
    lon = lax.axis_index("lon")
    ny = n_lat // nz
    y = lat // nz
    z = lat % nz
    points, width = grid.shape
    n_var = target.shape[1]
    piece = done.shape[0]
    nx = n_lon // 2
    x = lon // 2
    core = lon % 2
    x_rows = ny * piece
    half_rows = nx * x_rows
    grid_total = float(points * n_lat * n_lon)

    inner = 1 - 2 * core
    outer = -inner

    def wrap(value, count):
        value = jnp.where(value >= count, value - count, value)
        return jnp.where(value < 0, value + count, value)

    lats = {step: wrap(lat + step, n_lat) for step in (-1, 0, 1)}
    xs = [wrap(x + step, nx) for step in range(nx)]
    ys = [wrap(y + step, ny) for step in range(ny)]
    y_lats = [value * nz + z for value in ys]
    x_lons = [value * 2 + core for value in xs]
    z_lats = [y * nz + wrap(z + step, nz) for step in range(nz)]
    inner_lon = lon + inner
    outer_lon = wrap(lon + outer, n_lon)

    def near(lat_step, to_lon):
        return (lats[lat_step], to_lon)

    def at_xy(dx, dy):
        return (y_lats[dy], x_lons[dx])

    def at_z(step):
        return (z_lats[step], lon)

    def ring(count):
        return sorted(range(count), key=lambda d: (-min(d, count - d), d))

    xy_order = [(dx, dy) for dx in range(nx) for dy in range(ny) if dx or dy]
    xy_order.sort(key=lambda d: -(min(d[0], nx - d[0]) + min(d[1], ny - d[1])))
    z_order = [d for d in ring(nz) if d]

    peers = [near(step, to) for step in (1, -1) for to in (lon, outer_lon)]
    peers += [near(0, outer_lon), near(0, inner_lon)]
    peers += [at_xy(dx, dy) for dx, dy in xy_order]
    peers += [at_z(d) for d in z_order]

    def load(source, dest, slot):
        return pltpu.make_async_copy(source, dest, in_sem.at[slot])

    quarter = width // 4
    first = [
        load(w_enc_hbm.at[pl.ds(q * quarter, quarter)], w_f32.at[0, pl.ds(q * quarter, quarter)], q)
        for q in range(4)
    ]
    first += [
        load(grid_hbm.at[pl.ds(q * 128, 128)], grid.at[pl.ds(q * 128, 128)], 4 + q)
        for q in range(points // 128)
    ]
    later = [
        load(nbr_hbm, nbr, 6),
        load(m_idx_hbm, m_idx, 7),
        load(m_w_hbm, m_w, 8),
        load(w_dec_hbm, w_f32.at[1], 9),
        load(w_self_hbm.at[0], w_f32.at[2], 10),
        load(w_nbr_hbm.at[0], w_f32.at[3], 11),
        load(w_self_hbm.at[1], w_f32.at[4], 12),
        load(w_nbr_hbm.at[1], w_f32.at[5], 13),
        load(w_out_hbm, w_out, 14),
        load(target_hbm, target, 15),
        load(g_idx_hbm, g_idx, 16),
        load(g_w_hbm, g_w, 17),
        load(vw_hbm, vw, 18),
    ]
    for copy in first:
        copy.start()

    barrier = pltpu.get_barrier_semaphore()
    for peer in peers:
        pl.semaphore_signal(barrier, inc=1, device_id=peer, device_id_type=MESH)

    def split_weight(which, start=0, count=8):
        def body(step, carry):
            rows = span(step, width // 8)
            high, low = split(w_f32[which, rows, :])
            w_bf[which, 0, rows, :] = high
            w_bf[which, 1, rows, :] = low
            return carry

        lax.fori_loop(start, start + count, body, 0)

    def weight(which):
        return w_bf[which, 0], w_bf[which, 1]

    def locate(index, rows):
        shift = rows.bit_length() - 1
        lon_shift = n_lon.bit_length() - 1
        owner = index >> shift
        within = index & (rows - 1)
        band_slot = (owner >> lon_shift) - lat + 1
        tile_slot = ((owner & (n_lon - 1)) - lon + 1 + n_lon) & (n_lon - 1)
        lone = jnp.where(tile_slot == 1, 0, 1 + (tile_slot >> 1))
        other = jnp.where(tile_slot == 1, 3 + (band_slot >> 1), (band_slot & 2) + (tile_slot >> 1))
        far = jnp.where((band_slot == 1) | (tile_slot == 1), 0, lanes(5 * rows))
        return (jnp.where(band_slot == 1, lone, other) << shift) + within + far

    def select(local, factors, columns):
        place = lax.broadcasted_iota(jnp.int32, (local.shape[0], columns), 1)
        chosen = jnp.zeros((local.shape[0], columns), F32)
        for k in range(local.shape[1]):
            value = 1.0 if factors is None else factors[:, k : k + 1]
            chosen = chosen + jnp.where(place == local[:, k : k + 1], value, 0.0)
        return chosen

    def send(win, rows, turn, source, dest, group, peer):
        pltpu.make_async_remote_copy(
            src_ref=win.at[span(source, rows)],
            dst_ref=win.at[span(dest, rows)],
            send_sem=halo_send.at[turn],
            recv_sem=halo_recv.at[turn, group],
            device_id=peer,
            device_id_type=MESH,
        ).start()

    def lon_slot(step):
        return 1 + (step + 1) // 2

    def lat_slot(step):
        return 3 + (step + 1) // 2

    def corner(lat_step, lon_step):
        return 5 + (lat_step + 1) + (lon_step + 1) // 2

    def halo_start(win, rows, turn):
        for step in (1, -1):
            send(win, rows, turn, 0, lat_slot(-step), lat_slot(-step) - 2, near(step, lon))
        for step in (1, -1):
            send(win, rows, turn, 0, corner(-step, -outer), 3, near(step, outer_lon))
        send(win, rows, turn, 0, lon_slot(-outer), 0, near(0, outer_lon))
        send(win, rows, turn, 0, lon_slot(-inner), 0, near(0, inner_lon))

    def halo_wait(win, rows, turn, group, count):
        part = win.at[pl.ds(0, count * rows)]
        pltpu.make_async_copy(part, part, halo_recv.at[turn, group]).wait()

    def halo_forward(win, rows, turn):
        for step in (-1, 1):
            halo_wait(win, rows, turn, lat_slot(step) - 2, 1)
            send(win, rows, turn, lat_slot(step), corner(step, -inner), 3, near(0, inner_lon))

    def halo_inner(win, rows, turn):
        halo_wait(win, rows, turn, 0, 2)
        return split(win[0 : 5 * rows, :])

    def halo_corners(win, rows, turn):
        halo_wait(win, rows, turn, 3, 4)
        return split(win[5 * rows : 9 * rows, :])

    def columns(parts, start, stop):
        return tuple(part[:, start:stop] for part in parts)

    def halo_sent(win, rows, turn):
        part = win.at[pl.ds(0, 8 * rows)]
        pltpu.make_async_copy(part, part, halo_send.at[turn]).wait()

    blocks_dev = points // BS
    mesh_dev = nbr.shape[1]
    for q in range(4):
        first[q].wait()
        split_weight(0, 2 * q, 2)
    for copy in later:
        copy.start()
    for copy in first[4:]:
        copy.wait()

    def encode(step, carry):
        rows = span(step, 128)
        value = grid[rows, :]
        h_one = value + silu(mm3(split(value), weight(0)))
        high, low = split(h_one)
        h_bf[0, rows, :] = high
        h_bf[1, rows, :] = low
        means = jnp.sum(h_one.reshape(128 // BS, BS, width), axis=1) * (1.0 / BS)
        start = pl.multiple_of(step * (128 // BS), 128 // BS)
        win0[pl.ds(start, 128 // BS), :] = means
        return carry

    lax.fori_loop(0, points // 128, encode, 0)
    pl.semaphore_wait(barrier, len(peers))
    halo_start(win0, blocks_dev, 0)

    later[10].wait()
    later[11].wait()
    g_weights = g_w[...].T
    g_local = locate(g_idx[...].T, blocks_dev)
    g_far = lanes(5 * blocks_dev)
    g_select = split(select(g_local, g_weights, g_far + 4 * blocks_dev))
    g_total = jnp.sum(g_weights, axis=1, keepdims=True)
    later[0].wait()
    far = lanes(5 * mesh_dev)
    a_select = select(locate(nbr[...].T, mesh_dev), None, far + 4 * mesh_dev).astype(BF16)
    later[4].wait()
    split_weight(2)
    later[5].wait()
    split_weight(3)
    halo_forward(win0, blocks_dev, 0)
    cut = 5 * blocks_dev
    mesh = mm3(columns(g_select, 0, cut), halo_inner(win0, blocks_dev, 0))
    mesh = mesh + mm3(columns(g_select, g_far, g_far + 4 * blocks_dev), halo_corners(win0, blocks_dev, 0))
    mesh = mesh / g_total

    def hidden_part(step, carry):
        rows = span(step, 128)
        h_dec[rows, :] = mm3((h_bf[0, rows, :], h_bf[1, rows, :]), weight(1))
        return carry

    def gather(parts):
        high, low = parts[1]
        return dot(parts[0], high) + dot(parts[0], low)

    cut = 5 * mesh_dev
    wins = (win1, win2, win3)

    def own(win):
        return pl.ds(0, mesh_dev)

    for layer in range(L):
        win = wins[layer]
        win[own(win), :] = mesh
        halo_start(win, mesh_dev, layer + 1)
        center = mesh - jnp.mean(mesh, axis=1, keepdims=True)
        spread = jnp.mean(center * center, axis=1, keepdims=True)
        nrm = center / jnp.sqrt(spread + EPS)
        self_part = mm3(split(nrm), weight(2 + 2 * layer))
        if layer == 0:
            halo_forward(win, mesh_dev, layer + 1)
            for ready, which in ((6, 4), (7, 5)):
                later[ready].wait()
                split_weight(which)
            later[3].wait()
            split_weight(1)
            later[1].wait()
            later[2].wait()
            factors = m_w[...].T
            m_w_cols[...] = factors / jnp.sum(factors, axis=1, keepdims=True)
            m_idx_cols[...] = locate(m_idx[...].T, mesh_dev)

            def build(step, carry):
                rows = span(step, 64)
                chosen = select(m_idx_cols[rows, :], m_w_cols[rows, :], far + 4 * mesh_dev)
                high, low = split(chosen)
                back_bf[0, rows, :] = high
                back_bf[1, rows, :] = low
                return carry

            lax.fori_loop(0, points // 64, build, 0)
        else:
            lax.fori_loop(0, points // 128, hidden_part, 0)
            halo_forward(win, mesh_dev, layer + 1)
        agg = gather((a_select[:, :cut], halo_inner(win, mesh_dev, layer + 1)))
        agg = agg + gather((a_select[:, far:], halo_corners(win, mesh_dev, layer + 1)))
        agg = agg / float(nbr.shape[0])
        mesh = mesh + silu(self_part + mm3(split(agg), weight(3 + 2 * layer)))

    win3[own(win3), :] = mm3(split(mesh), weight(1))
    halo_start(win3, mesh_dev, 3)
    later[8].wait()
    high, low = split(w_out[...])
    w_out_bf[0] = high
    w_out_bf[1] = low
    halo_forward(win3, mesh_dev, 3)
    later[9].wait()
    power = jnp.sum(target[...] * target[...], axis=0, keepdims=True)
    later[12].wait()
    weights = vw[...].astype(F32)
    wsum = jnp.sum(weights, axis=1, keepdims=True)
    table = halo_inner(win3, mesh_dev, 3)
    for step in range(points // 128):
        rows = pl.ds(step * 128, 128)
        h_dec[rows, :] += mm3((back_bf[0, rows, 0:cut], back_bf[1, rows, 0:cut]), table)
    table = halo_corners(win3, mesh_dev, 3)
    w_out_parts = (w_out_bf[0], w_out_bf[1])
    err = jnp.zeros((1, n_var), F32)
    for step in range(points // 128):
        rows = pl.ds(step * 128, 128)
        corners = (back_bf[0, rows, pl.ds(far, 4 * mesh_dev)], back_bf[1, rows, pl.ds(far, 4 * mesh_dev)])
        hidden = silu(h_dec[rows, :] + mm3(corners, table))
        hh, hl = split(hidden)
        out = mm3((hh, hl), w_out_parts)
        pred[rows, :] = out
        resid = out - target[rows, :]
        err = err + jnp.sum(resid * resid, axis=0, keepdims=True)
        h_bf[0, rows, :] = hh
        h_bf[1, rows, :] = hl
        high, low = split(resid)
        resid_bf[0, rows, :] = high
        resid_bf[1, rows, :] = low

    def grad_half(start):
        rows = pl.ds(pl.multiple_of(start, half_rows), half_rows)
        left = (h_bf[0, :, rows].T, h_bf[1, :, rows].T)
        grad[rows, :] = mm3(left, (resid_bf[0], resid_bf[1]))
        return rows

    def push(source, dest, stage, recv, peer):
        pltpu.make_async_remote_copy(
            src_ref=source,
            dst_ref=dest,
            send_sem=ar_send.at[stage],
            recv_sem=recv,
            device_id=peer,
            device_id_type=MESH,
        ).start()

    def drain(part, sem):
        pltpu.make_async_copy(part, part, sem).wait()

    partner = near(0, inner_lon)
    me = x * ny + y
    keep_row = core * half_rows

    st0[core] = jnp.concatenate([power, err], axis=0)
    push(st0.at[core], st0.at[core], 0, ar_recv.at[0], partner)
    given = grad_half((1 - core) * half_rows)
    push(grad.at[given], half, 1, half_recv.at[0], partner)
    kept = grad_half(keep_row)
    pred_copy = pltpu.make_async_copy(pred, pred_out, out_sem.at[0])
    pred_copy.start()

    drain(st0.at[pl.ds(0, 1)], ar_recv.at[0])
    s1_src[:, piece : piece + 2, :] = jnp.broadcast_to((st0[0] + st0[1])[None], (nx * ny, 2, n_var))
    drain(half, half_recv.at[0])
    s1_src[:, 0:piece, :] = (grad[kept, :] + half[...]).reshape(nx * ny, piece, n_var)
    for dx, dy in xy_order:
        push(s1_src.at[xs[dx] * ny + ys[dy]], s1.at[me], 2, ar_recv.at[1], at_xy(dx, dy))
    s1[me] = s1_src[me]

    others = nx * ny - 1
    drain(s1.at[pl.ds(0, others)], ar_recv.at[1])
    s2[z] = jnp.sum(s1[...], axis=0)
    for d in z_order:
        push(s2.at[z], s2.at[z], 3, ar_recv.at[2], at_z(d))

    drain(s2.at[pl.ds(0, nz - 1)], ar_recv.at[2])
    value = jnp.sum(s2[...], axis=0)
    stats = value[piece : piece + 2]
    scale = stats[0:1] / grid_total + 1e-06
    norm = scale * grid_total * wsum
    coef = 2.0 * weights / norm

    mine = pl.ds(pl.multiple_of(keep_row + me * piece, piece), piece)
    done[...] = value[0:piece] * coef
    for dx, dy in xy_order:
        push(done, grad_out.at[mine], 4, part_recv.at[x], at_xy(dx, dy))
    loss = jnp.sum(weights * stats[1:2] / norm, axis=1, keepdims=True)
    loss_row[...] = jnp.broadcast_to(loss, loss_row.shape)
    loss_copy = pltpu.make_async_copy(loss_row, loss_out, out_sem.at[1])
    loss_copy.start()
    done_copy = pltpu.make_async_copy(done, grad_out.at[mine], out_sem.at[2])
    done_copy.start()
    done_copy.wait()
    for dx in reversed(ring(nx)):
        bx = xs[dx]
        rows = pl.ds(pl.multiple_of(keep_row + bx * x_rows, x_rows), x_rows)
        count = ny - 1 if dx == 0 else ny
        drain(grad_out.at[pl.ds(0, count * piece)], part_recv.at[bx])
        push(grad_out.at[rows], grad_out.at[rows], 5, ar_recv.at[3], partner)
    drain(grad_out.at[pl.ds(0, half_rows)], ar_recv.at[3])

    halo_sent(win0, blocks_dev, 0)
    for turn, win in enumerate(wins):
        halo_sent(win, mesh_dev, turn + 1)
    drain(st0.at[pl.ds(0, 1)], ar_send.at[0])
    drain(grad.at[pl.ds(0, half_rows)], ar_send.at[1])
    drain(s1.at[pl.ds(0, others)], ar_send.at[2])
    drain(s2.at[pl.ds(0, nz - 1)], ar_send.at[3])
    drain(grad_out.at[pl.ds(0, others * piece)], ar_send.at[4])
    drain(grad_out.at[pl.ds(0, half_rows)], ar_send.at[5])
    pred_copy.wait()
    loss_copy.wait()


def shards(
    nz,
    grid_in,
    target,
    w_enc,
    w_mix_self,
    w_mix_nbr,
    w_dec,
    w_out,
    var_weight,
    g2m_idx,
    g2m_w,
    mesh_nbr,
    m2g_idx,
    m2g_w,
):
    n_lat = lax.axis_size("lat")
    n_lon = lax.axis_size("lon")
    ny = n_lat // nz
    points, width = grid_in.shape
    n_var = target.shape[1]
    mesh_dev = mesh_nbr.shape[0]
    turned = (g2m_idx.T, g2m_w.T, mesh_nbr.T, m2g_idx.T, m2g_w.T)
    blocks_dev = points // BS
    piece = width // (n_lon * ny)
    window = 9 * mesh_dev
    vw = var_weight.reshape(1, n_var)
    operands = (grid_in, target, w_enc, w_mix_self, w_mix_nbr, w_dec, w_out, vw, *turned)
    hbm = pl.BlockSpec(memory_space=pl.ANY)
    pred, loss, grad = pl.pallas_call(
        functools.partial(program_kernel, n_lat, n_lon, nz),
        name="forecast_step",
        out_shape=(
            jax.ShapeDtypeStruct((points, n_var), F32),
            jax.ShapeDtypeStruct((1, n_var), F32),
            jax.ShapeDtypeStruct((width, n_var), F32),
        ),
        in_specs=[hbm] * len(operands),
        out_specs=(hbm, hbm, hbm),
        scratch_shapes=[
            pltpu.VMEM((points, width), F32),
            pltpu.VMEM((points, n_var), F32),
            pltpu.VMEM((6, width, width), F32),
            pltpu.VMEM((width, n_var), F32),
            pltpu.VMEM((1, n_var), jnp.int32),
            *[pltpu.VMEM(a.shape, a.dtype) for a in turned],
            pltpu.VMEM(m2g_idx.shape, jnp.int32),
            pltpu.VMEM(m2g_w.shape, F32),
            pltpu.VMEM((6, 2, width, width), BF16),
            pltpu.VMEM((2, width, n_var), BF16),
            pltpu.VMEM((2, points, width), BF16),
            pltpu.VMEM((2, points, n_var), BF16),
            pltpu.VMEM((points, width), F32),
            pltpu.VMEM((2, points, lanes(5 * mesh_dev) + 4 * mesh_dev), BF16),
            pltpu.VMEM((9 * blocks_dev, width), F32),
            pltpu.VMEM((window, width), F32),
            pltpu.VMEM((window, width), F32),
            pltpu.VMEM((window, width), F32),
            pltpu.VMEM((points, n_var), F32),
            pltpu.VMEM((width, n_var), F32),
            pltpu.VMEM((width // 2, n_var), F32),
            pltpu.VMEM((n_lon // 2 * ny, piece + 2, n_var), F32),
            pltpu.VMEM((n_lon // 2 * ny, piece + 2, n_var), F32),
            pltpu.VMEM((nz, piece + 2, n_var), F32),
            pltpu.VMEM((piece, n_var), F32),
            pltpu.VMEM((1, n_var), F32),
            pltpu.VMEM((2, 2, n_var), F32),
            pltpu.SemaphoreType.DMA((19,)),
            pltpu.SemaphoreType.DMA((3,)),
            pltpu.SemaphoreType.DMA((4, 4)),
            pltpu.SemaphoreType.DMA((4,)),
            pltpu.SemaphoreType.DMA((1,)),
            pltpu.SemaphoreType.DMA((n_lon // 2,)),
            pltpu.SemaphoreType.DMA((4,)),
            pltpu.SemaphoreType.DMA((6,)),
        ],
        compiler_params=pltpu.CompilerParams(
            collective_id=0, has_side_effects=True, vmem_limit_bytes=28 << 20
        ),
    )(*[pltpu.with_memory_space_constraint(a, pltpu.HBM) for a in operands])
    pred, grad = pl.pallas_call(
        place_kernel,
        name="place",
        out_shape=(
            jax.ShapeDtypeStruct((points, n_var), F32),
            jax.ShapeDtypeStruct((width, n_var), F32),
        ),
        in_specs=[hbm] * 2,
        out_specs=(hbm, hbm),
        scratch_shapes=[pltpu.SemaphoreType.DMA((2,))],
        compiler_params=pltpu.CompilerParams(vmem_limit_bytes=1 << 20),
    )(pred, grad)
    return (pred, loss[0, 0], grad)


def solution(mesh, nz=NZ):
    rows = P(("lat", "lon"), None)
    placed = (rows, rows, P(), P(), P(), P(), P(), P(), rows, rows, rows, rows, rows)
    return jax.shard_map(
        functools.partial(shards, nz),
        mesh=mesh,
        in_specs=placed,
        out_specs=(rows, P(), P()),
        check_vma=False,
    )
```
